32 devices in a mesh: expert: 4 (over x, core), wshard: 8 (over z, y).
Axes of the slice: x: 2, y: 2, z: 4, core: 2. Of those that a mesh axis runs over, the one named last changes fastest.
Arguments:
- tokens: bfloat16 [4096, 2048], P(('expert', 'wshard')), may hold values from -48 to 48
- segment_ids: int32 [4096], P('expert'), may hold values from 0 to 15, never falling along the last dimension, each value on 1 to 512 neighbouring positions
- routes: int32 [4096, 4], P(('expert', 'wshard')), may hold values from 0 to 7, all different within a row; in each aligned block of 128 rows (0 to 127, 128 to 255, ...) at most 128 rows name the same one
- attn_gain: float32 [2048], replicated, may hold values from 0.5 to 1.5
- query_weight: bfloat16 [2048, 2048], P('wshard'), may hold values from -0.125 to 0.125
- key_weight: bfloat16 [2048, 2048], P('wshard'), may hold values from -0.125 to 0.125
- value_weight: bfloat16 [2048, 2048], P('wshard'), may hold values from -0.125 to 0.125
- out_weight: bfloat16 [2048, 2048], P('wshard'), may hold values from -1 to 1
- query_gain: float32 [128], replicated, may hold values from 0.5 to 1.5
- key_gain: float32 [128], replicated, may hold values from 0.5 to 1.5
- ffn_gain: float32 [2048], replicated, may hold values from 0.5 to 1.5
- router_weight: bfloat16 [2048, 8], replicated, may hold values from -0.25 to 0.25
- gate_weight: bfloat16 [8, 2048, 1024], P('expert', 'wshard'), may hold values from -0.125 to 0.125
- up_weight: bfloat16 [8, 2048, 1024], P('expert', 'wshard'), may hold values from -0.125 to 0.125
- down_weight: bfloat16 [8, 1024, 2048], P('expert', None, 'wshard'), may hold values from -0.375 to 0.375
- d_output: bfloat16 [4096, 2048], P(('expert', 'wshard')), may hold values from -6 to 6
Outputs:
- output: bfloat16 [4096, 2048], P(('expert', 'wshard'))
- tokens_grad: bfloat16 [4096, 2048], P(('expert', 'wshard'))
- attn_gain_grad: float32 [2048], replicated
- query_weight_grad: float32 [2048, 2048], P('wshard')
- key_weight_grad: float32 [2048, 2048], P('wshard')
- value_weight_grad: float32 [2048, 2048], P('wshard')
- out_weight_grad: float32 [2048, 2048], P('wshard')
- query_gain_grad: float32 [128], replicated
- key_gain_grad: float32 [128], replicated
- ffn_gain_grad: float32 [2048], replicated
- router_weight_grad: float32 [2048, 8], replicated
- gate_weight_grad: float32 [8, 2048, 1024], P('expert', 'wshard')
- up_weight_grad: float32 [8, 2048, 1024], P('expert', 'wshard')
- down_weight_grad: float32 [8, 1024, 2048], P('expert', None, 'wshard')
- stream_rms: float32 [4], replicated
The draws below stay inside these ranges and needn't reach their ends.
Inputs may be any that keep to these rules, and one draw needn't show every extreme that they name: `routes`: each row names 4 different experts. Among the 128 rows of one device no expert is named more than 128 times, a bound that some block reaches. `segment_ids`: segment numbers never fall along the tokens; a segment holds 1 to 512 tokens, and some segment holds exactly 512.
All inputs are finite; a program needn't handle non-finite values.
Results may differ from the reference program's by a relative error of at most 0.023.
Values may be sent and summed in bfloat16 or wider, within the bound.
No kernel may reach another device: no remote copies, remote signals or barrier semaphores. Data moves between devices by JAX's collectives and lax.ppermute only.
A program may use at most 384 MiB of HBM per device.

```python
import math
import jax
import jax.numpy as jnp
import numpy as np
from jax import lax

D = 2048
HEADS = 16
HEAD_DIM = 128
FF = 1024
TOPK = 4
EXPERTS = 8
TOK_DEV = 128
CAP = 128
SEQ = 1024
TOKENS = 4096
N_EXPERT = 4


def draw_tokens(key, part):
    subkeys = jax.random.split(key, 3)
    position = jnp.arange(TOKENS, dtype=jnp.float32)[:, None]
    rising = jnp.exp(math.log(3.0) * position / TOKENS)
    columns = jnp.exp(jax.random.uniform(subkeys[1], (1, D), jnp.float32, math.log(0.4), math.log(4.0)))
    roughness = jnp.exp(jax.random.uniform(subkeys[2], (TOKENS, 1), jnp.float32, math.log(0.6), math.log(1.6)))
    values = jnp.clip(jax.random.normal(subkeys[0], (TOKENS, D), jnp.float32), -4.0, 4.0)
    return (0.6 * values * columns * roughness * rising).astype(jnp.bfloat16)


def block_scale(stream_key, dims, cuts, least, high):
    level, own = 1.0, jax.random.fold_in(stream_key, 6)
    for dim, parts in cuts:
        steps = jnp.exp(jax.random.uniform(jax.random.fold_in(own, dim), (parts,), jnp.float32, least / len(cuts), high / len(cuts)))
        level = level * jnp.repeat(steps, dims[dim] // parts).reshape([-1 if axis == dim else 1 for axis in range(len(dims))])
    return level


def profile(count, total, most, slope):
    loads = [(1 << 20) // math.isqrt(rank ** slope) + 1 for rank in range(2, count + 1)]
    surplus, counts = total - most - (count - 1), [1] * (count - 1)
    while surplus > 0:
        candidates = [i for i in range(count - 1) if counts[i] < most]
        whole, budget = sum([loads[i] for i in candidates]), surplus
        for i in candidates:
            addition = min(most - counts[i], max(1, budget * loads[i] // whole), surplus)
            counts[i] = counts[i] + addition
            surplus = surplus - addition
    return np.array([most] + counts)


def uneven(rng, amount, total, bound, skew):
    if amount == 2:
        one = jax.random.randint(rng, (), max(1, total - bound), min(bound, total - 1) + 1)
        return jnp.stack([one, total - one])
    sizes = jnp.asarray(profile(amount, total, bound, skew), jnp.int32)
    couples = (amount - 1) // 2
    donor, receiver = sizes[1:1 + 2 * couples:2], sizes[2:2 + 2 * couples:2]
    slack = jnp.minimum(donor - 1, bound - receiver)
    moved = jax.random.randint(jax.random.fold_in(rng, 1), (couples,), 0, 1 << 20) % (slack + 1)
    sizes = sizes.at[1:1 + 2 * couples:2].set(donor - moved).at[2:2 + 2 * couples:2].set(receiver + moved)
    return sizes[jax.random.permutation(jax.random.fold_in(rng, 2), amount)]


def deal_out(rng, own, number, rows, count, top, most, skew):
    sequence = jax.random.permutation(rng, count)
    heavy_load, ordinary = load_shares(count, rows * top, most, skew, True), load_shares(count, rows * top, most, skew, False)
    places = jnp.arange(count)

    def named(lengths, offset_by):
        used = int((lengths > 0).sum())
        fixed = max(1, used // 4)
        moved = fixed + (places - fixed + offset_by * (used - fixed)) % max(1, count - fixed)
        return jnp.zeros((count,), jnp.int32).at[sequence[jnp.where(places < fixed, places, moved)]].set(jnp.asarray(lengths, jnp.int32))

    lengths = jnp.where(number % 4 == 0, named(heavy_load, number // 4), named(ordinary, number - number // 4 - 1))
    mixed = jax.random.permutation(jax.random.fold_in(own, 3), count)
    donor, taker = mixed[0:count // 2 * 2:2], mixed[1:count // 2 * 2:2]
    margin = jnp.minimum(lengths[donor] - 1, most - lengths[taker]) // 2
    margin = jnp.where((donor == sequence[0]) | (taker == sequence[0]) | (lengths[taker] == 0), 0, jnp.maximum(margin, 0))
    moved = jax.random.randint(jax.random.fold_in(own, 4), (count // 2,), 0, 1 << 20) % (margin + 1)
    lengths = lengths.at[donor].add(-moved).at[taker].add(moved)
    labels = jnp.searchsorted(jnp.cumsum(lengths), jnp.arange(rows * top), side="right").astype(jnp.int32)
    table = labels.reshape(top, rows).T
    table = table[jax.random.permutation(jax.random.fold_in(own, 1), rows)]
    offset_by = jax.random.randint(jax.random.fold_in(own, 2), (rows, 1), 0, top)
    return jnp.take_along_axis(table, (jnp.arange(top)[None, :] + offset_by) % top, axis=1)


def load_shares(count, total, reach, skew, full):
    loads = [(1 << 20) // math.isqrt(grade ** skew) + 1 for grade in range(1, count + 1)]
    largest = reach if full else min(reach, max(-(-total // count), total * loads[0] // sum(loads)))
    least = 1 if total - largest >= count - 1 else 0
    holding, rest = [largest] + [least] * (count - 1), total - largest - least * (count - 1)
    while rest > 0:
        movable = [i for i in range(1, count) if holding[i] < largest] or [i for i in range(1, count) if holding[i] < reach]
        mass, left = sum([loads[i] for i in movable]), rest
        for i in movable:
            addition = min(reach - holding[i], max(1, left * loads[i] // mass), rest)
            holding[i] = holding[i] + addition
            rest = rest - addition
    return np.array(holding)


def centred(own_key, dims, scale, reach, pieces=(), held_as=jnp.bfloat16):
    values = scale * jax.random.normal(own_key, dims, jnp.float32)
    if pieces:
        values = values * block_scale(own_key, dims, pieces, -0.22, 0.18)
    return jnp.clip(values, -reach, reach).astype(held_as)


def setup_inputs(seed: int = 0) -> dict:
    key_of = jax.random.split(jax.random.key(seed), 17)
    tokens = draw_tokens(jax.random.fold_in(key_of[16], 71), 0)
    segment_ids = jnp.searchsorted(jnp.cumsum(uneven(key_of[1], 4 * N_EXPERT, TOKENS, SEQ // 2, 1)), jnp.arange(TOKENS), side="right").astype(jnp.int32)
    routes_keys = jax.random.split(jax.random.fold_in(key_of[2], 1), TOKENS // TOK_DEV)
    routes_turns = jax.random.permutation(jax.random.fold_in(key_of[2], 3), TOKENS // TOK_DEV)
    routes = jax.vmap(lambda own, number: deal_out(jax.random.fold_in(key_of[2], 2), own, number, TOK_DEV, EXPERTS, TOPK, CAP, 2))(routes_keys, routes_turns).reshape((TOKENS, TOPK))
    attn_gain = jnp.clip(1.0 + 0.1 * jax.random.normal(key_of[3], (D,), jnp.float32), 0.5, 1.5)
    query_weight = centred(key_of[4], (D, D), D ** -0.5, 0.125, ((0, 8),))
    key_weight = centred(key_of[5], (D, D), D ** -0.5, 0.125, ((0, 8),))
    value_weight = centred(key_of[6], (D, D), D ** -0.5, 0.125, ((0, 8),))
    out_weight = centred(key_of[7], (D, D), (D // 64) ** -0.5, 1.0, ((0, 8),))
    query_gain = jnp.clip(1.0 + 0.1 * jax.random.normal(key_of[8], (HEAD_DIM,), jnp.float32), 0.5, 1.5)
    key_gain = jnp.clip(1.0 + 0.1 * jax.random.normal(key_of[9], (HEAD_DIM,), jnp.float32), 0.5, 1.5)
    ffn_gain = jnp.clip(1.0 + 0.1 * jax.random.normal(key_of[10], (D,), jnp.float32), 0.5, 1.5)
    router_weight = centred(key_of[11], (D, EXPERTS), (D // 4) ** -0.5, 0.25)
    gate_weight = centred(key_of[12], (EXPERTS, D, FF), D ** -0.5, 0.125, ((0, 4), (1, 8)))
    up_weight = centred(key_of[13], (EXPERTS, D, FF), D ** -0.5, 0.125, ((0, 4), (1, 8)))
    down_weight = centred(key_of[14], (EXPERTS, FF, D), (FF // 4) ** -0.5, 0.375, ((0, 4), (2, 8)))
    d_output = centred(key_of[15], (TOKENS, D), 1.0, 6.0, ((0, 32),))
    return dict(tokens=tokens, segment_ids=segment_ids, routes=routes, attn_gain=attn_gain, query_weight=query_weight, key_weight=key_weight, value_weight=value_weight, out_weight=out_weight, query_gain=query_gain, key_gain=key_gain, ffn_gain=ffn_gain, router_weight=router_weight, gate_weight=gate_weight, up_weight=up_weight, down_weight=down_weight, d_output=d_output)


epsilon = 1e-06
rope_base = 50000.0
highest = lax.Precision.HIGHEST

@jax.custom_vjp
def low(v):
    return lax.optimization_barrier(v.astype(jnp.bfloat16)).astype(jnp.float32)

@jax.custom_vjp
def low_back(v):
    return v

def low_keep(v):
    return (low(v), None)

def low_pass(kept, grad):
    return (grad,)

def back_keep(v):
    return (v, None)

def back_low(kept, grad):
    return (low(grad),)
low.defvjp(low_keep, low_pass)
low_back.defvjp(back_keep, back_low)

def both_ways(values):
    return low(low_back(values))

def exact_dot(first_operand, second_operand):
    return jnp.dot(first_operand, second_operand, precision=highest)

def norm_rows(values, gain_vector):
    return values * lax.rsqrt(lax.optimization_barrier(jnp.mean(values * values, axis=-1, keepdims=True)) + epsilon) * gain_vector

def rope_tables(positions):
    half_dim = HEAD_DIM // 2
    frequency = rope_base ** (-2.0 * jnp.arange(half_dim, dtype=jnp.float32) / HEAD_DIM)
    angles = positions.astype(jnp.float32)[:, None] * frequency[None, :]
    return (jnp.cos(angles)[:, None, :], jnp.sin(angles)[:, None, :])

def rotate(values, cosine_table, sine_table):
    half_dim = values.shape[-1] // 2
    first_half = values[..., :half_dim]
    second_half = values[..., half_dim:]
    return jnp.concatenate([first_half * cosine_table - second_half * sine_table, second_half * cosine_table + first_half * sine_table], axis=-1)

def attend(inputs):
    queries, keys_all, values_all, segments = inputs
    scores = jnp.einsum('qd,kd->qk', queries, keys_all, precision=highest) / math.sqrt(HEAD_DIM)
    scores = low_back(scores)
    same_segment = segments[:, None] == segments[None, :]
    scores = jnp.where(same_segment, scores, -1e+30)
    attn_probs = jax.nn.softmax(scores, axis=-1)
    return jnp.einsum('qk,kd->qd', low(attn_probs), values_all, precision=highest)

def block_experts(block_item, gate_weight, up_weight, down_weight):
    rows_in, mixing, chosen = block_item
    flat_routes = chosen.reshape(-1)
    route_count = flat_routes.shape[0]
    experts = gate_weight.shape[0]
    capacity = CAP
    expert_hits = (flat_routes[:, None] == jnp.arange(experts, dtype=jnp.int32)[None, :]).astype(jnp.int32)
    slot_index = lax.optimization_barrier(jnp.sum((jnp.cumsum(expert_hits, axis=0) - 1) * expert_hits, axis=1)).astype(jnp.int32)
    slot_table = jnp.full((experts, capacity), route_count, jnp.int32).at[flat_routes, slot_index].set(jnp.arange(route_count, dtype=jnp.int32))
    filled = (slot_table < route_count)[..., None]
    owners = jnp.minimum(slot_table, route_count - 1) // TOPK
    picked = low_back(jnp.where(filled, rows_in[owners], 0.0))
    gate_pre = low_back(jnp.einsum('ecd,edf->ecf', picked, gate_weight, precision=highest))
    up_pre = low_back(jnp.einsum('ecd,edf->ecf', picked, up_weight, precision=highest))
    hidden = low(jax.nn.silu(gate_pre) * up_pre)
    produced = both_ways(jnp.einsum('ecf,efd->ecd', hidden, down_weight, precision=highest))
    routed = produced[flat_routes, slot_index].reshape(TOK_DEV, TOPK, -1)
    return jnp.einsum('tk,tkd->td', mixing, routed, precision=highest)

def reference(tokens, segment_ids, routes, attn_gain, query_weight, key_weight, value_weight, out_weight, query_gain, key_gain, ffn_gain, router_weight, gate_weight, up_weight, down_weight, d_output):
    cosine_table, sine_table = rope_tables(jnp.arange(TOKENS, dtype=jnp.int32) % SEQ)
    head_segments = jnp.repeat(segment_ids.reshape(N_EXPERT, SEQ), HEADS, axis=0)

    def per_head(values):
        return values.reshape(N_EXPERT, SEQ, HEADS, HEAD_DIM).transpose(0, 2, 1, 3).reshape(N_EXPERT * HEADS, SEQ, HEAD_DIM)

    def forward(stream, attn_gain, query_weight, key_weight, value_weight, out_weight, query_gain, key_gain, ffn_gain, router_weight, gate_weight, up_weight, down_weight):
        normed = low(norm_rows(stream, attn_gain))
        query_raw = low_back(exact_dot(normed, query_weight)).reshape(TOKENS, HEADS, HEAD_DIM)
        key_raw = low_back(exact_dot(normed, key_weight)).reshape(TOKENS, HEADS, HEAD_DIM)
        value_rows = both_ways(exact_dot(normed, value_weight)).reshape(TOKENS, HEADS, HEAD_DIM)
        queries = low(rotate(norm_rows(query_raw, query_gain), cosine_table, sine_table))
        keys_all = low(rotate(norm_rows(key_raw, key_gain), cosine_table, sine_table))
        mixed_rows = lax.map(jax.checkpoint(attend), (per_head(queries), per_head(keys_all), per_head(value_rows), head_segments))
        mixed_rows = mixed_rows.reshape(N_EXPERT, HEADS, SEQ, HEAD_DIM).transpose(0, 2, 1, 3).reshape(TOKENS, D)
        attended = low_back(exact_dot(both_ways(mixed_rows), out_weight))
        middle = stream + attended
        ffn_in = low(norm_rows(middle, ffn_gain))
        logits = exact_dot(ffn_in, router_weight)
        mixing = jax.nn.softmax(jnp.take_along_axis(logits, routes, axis=1), axis=1)
        blocks = TOKENS // TOK_DEV
        expert_out = lax.map(jax.checkpoint(lambda block_item: block_experts(block_item, gate_weight, up_weight, down_weight)), (ffn_in.reshape(blocks, TOK_DEV, D), mixing.reshape(blocks, TOK_DEV, TOPK), routes.reshape(blocks, TOK_DEV, TOPK)))
        expert_out = expert_out.reshape(TOKENS, D)
        final_stream = middle + expert_out
        return (final_stream, (middle, attended, expert_out))
    floats = [array.astype(jnp.float32) for array in (tokens, attn_gain, query_weight, key_weight, value_weight, out_weight, query_gain, key_gain, ffn_gain, router_weight, gate_weight, up_weight, down_weight)]
    final_stream, pullback, extras = jax.vjp(forward, *floats, has_aux=True)
    gradients = pullback(d_output.astype(jnp.float32))
    middle, attended, expert_out = extras
    stream_rms = jnp.sqrt(jnp.stack([jnp.mean(middle * middle), jnp.mean(final_stream * final_stream), jnp.mean(attended * attended), jnp.mean(expert_out * expert_out)]))
    return (final_stream.astype(jnp.bfloat16), gradients[0].astype(jnp.bfloat16), gradients[1], gradients[2], gradients[3], gradients[4], gradients[5], gradients[6], gradients[7], gradients[8], gradients[9], gradients[10], gradients[11], gradients[12], stream_rms)
```

```python
import functools
import math

import jax
import jax.numpy as jnp
from jax import lax
from jax.experimental import pallas as pl
from jax.experimental.pallas import tpu as pltpu
from jax.sharding import PartitionSpec as P

HEADS = 16
HEAD_DIM = 128
epsilon = 1e-06
rope_base = 50000.0
highest = lax.Precision.HIGHEST
bf16 = jnp.bfloat16
f32 = jnp.float32

NN = (((1,), (0,)), ((), ()))
NT = (((1,), (1,)), ((), ()))
TN = (((0,), (0,)), ((), ()))


def mm(a, b, dims=NN):
    return lax.dot_general(a, b, dims, preferred_element_type=f32)


def ring_order(n):
    return list(range(0, n, 2)) + list(range(n - 1, 0, -2))


class Ring:
    def __init__(self, axis):
        self.axis = axis
        self.n = n = lax.axis_size(axis)
        order = ring_order(n)
        self.down = [(order[i], order[(i + 1) % n]) for i in range(n)]
        self.up = [(b, a) for a, b in self.down]
        place = [order.index(w) for w in range(n)]
        here = jnp.asarray(place, jnp.int32)[lax.axis_index(axis)]
        self.half = n // 2
        self.offsets = [0]
        for s in range(1, self.half):
            self.offsets += [-s, s]
        self.offsets.append(-self.half)
        table = jnp.asarray(order, jnp.int32)
        self.owner = table[(here + jnp.asarray(self.offsets, jnp.int32) + n) % n]

    def gather(self, own, far_up=False):
        got = {0: own}
        down = up = own
        for s in range(1, self.half + 1):
            if s < self.half or not far_up:
                down = lax.ppermute(down, self.axis, self.down)
                got[-s] = down
            if s < self.half or far_up:
                up = lax.ppermute(up, self.axis, self.up)
                got[s if s < self.half else -s] = up
        return [got[o] for o in self.offsets]

    def scatter(self, parts, far_up=False):
        part = dict(zip(self.offsets, parts))
        part[self.half] = part[-self.half]

        def chain(length, sign, perm):
            moving = part[sign * length]
            for s in range(length - 1, -1, -1):
                came = lax.ppermute(moving, self.axis, perm)
                if s:
                    moving = (came.astype(f32) + part[sign * s].astype(f32)).astype(bf16)
            return came.astype(f32)

        ahead = chain(self.half - (1 if far_up else 0), 1, self.down)
        behind = chain(self.half - (0 if far_up else 1), -1, self.up)
        return part[0].astype(f32) + ahead + behind


def bits_of(size):
    return [1 << b for b in range(size.bit_length() - 1)]


def swap(x, axis, bit):
    return lax.ppermute(x, axis, [(i, i ^ bit) for i in range(lax.axis_size(axis))])


def gather_bits(x, axis):
    index = lax.axis_index(axis)
    out = x[None]
    for bit in reversed(bits_of(lax.axis_size(axis))):
        came = swap(out, axis, bit)
        high = (index & bit) != 0
        out = jnp.stack([jnp.where(high, came, out), jnp.where(high, out, came)], axis=1)
        out = out.reshape((-1,) + x.shape)
    return out


def scatter_bits(x, axis):
    index = lax.axis_index(axis)
    for bit in bits_of(lax.axis_size(axis)):
        pairs = x.reshape((-1, 2) + x.shape[1:])
        high = (index & bit) != 0
        keep = jnp.where(high, pairs[:, 1], pairs[:, 0])
        came = swap(jnp.where(high, pairs[:, 0], pairs[:, 1]), axis, bit)
        x = (keep.astype(f32) + came.astype(f32)).astype(bf16)
    return x[0]


def sum_all(x):
    for axis in ("expert", "wshard"):
        for bit in bits_of(lax.axis_size(axis)):
            x = x + swap(x, axis, bit)
    return x


def relative(owners):
    rel = [0]
    for bit in reversed(bits_of(owners)):
        rel += [r ^ bit for r in rel]
    return rel


def gather_relative(x, axis):
    blocks = [x]
    for bit in reversed(bits_of(lax.axis_size(axis))):
        blocks += [swap(b, axis, bit) for b in blocks]
    return blocks


def scatter_relative(blocks, axis):
    for bit in bits_of(lax.axis_size(axis)):
        half = len(blocks) // 2
        came = [swap(b.astype(bf16), axis, bit) for b in blocks[half:]]
        blocks = [b + c.astype(f32) for b, c in zip(blocks[:half], came)]
    return blocks[0]


def expert_kernel(n, owner, x_ref, g_ref, m_ref, *refs):
    weights = refs[:n]
    y_ref, dx_ref, mg_ref = refs[n : n + 3]
    grads = refs[n + 3 :]
    depth = weights[0].shape[0] // 3

    @pl.when(pl.program_id(0) == 0)
    def _():
        y_ref[...] = jnp.zeros_like(y_ref)
        dx_ref[...] = jnp.zeros_like(dx_ref)
        mg_ref[...] = jnp.zeros_like(mg_ref)

    columns = [pl.ds(pl.multiple_of(owner[j] * depth, depth), depth) for j in range(n)]
    gate = up = back = None
    for j in range(n):
        x, g = x_ref[:, columns[j]], g_ref[:, columns[j]]
        a = mm(x, weights[j][:depth])
        b = mm(x, weights[j][depth : 2 * depth])
        c = mm(g, weights[j][2 * depth :])
        gate, up, back = (a, b, c) if j == 0 else (gate + a, up + b, back + c)
    sig = 1.0 / (1.0 + jnp.exp(-gate))
    act = gate * sig
    hidden = act * up
    mix = m_ref[...]
    mg_ref[...] += jnp.sum(hidden * back, axis=1, keepdims=True)
    mixed = (mix * hidden).astype(bf16)
    hidden_grad = mix * back
    gate_grad = (hidden_grad * up * sig * (1.0 + gate * (1.0 - sig))).astype(bf16)
    up_grad = (hidden_grad * act).astype(bf16)
    for j in range(n):
        x, g = x_ref[:, columns[j]], g_ref[:, columns[j]]
        y_ref[:, columns[j]] += mm(mixed, weights[j][2 * depth :], NT)
        dx_ref[:, columns[j]] += mm(gate_grad, weights[j][:depth], NT) + mm(
            up_grad, weights[j][depth : 2 * depth], NT
        )
        grads[j][:depth] = mm(x, gate_grad, TN).astype(bf16)
        grads[j][depth : 2 * depth] = mm(x, up_grad, TN).astype(bf16)
        grads[j][2 * depth :] = mm(g, mixed, TN).astype(bf16)


def expert_pass(owner, x, g, mix, weights, width=256):
    n = len(weights)
    rows, model = x.shape
    deep, hidden = weights[0].shape

    def full(columns):
        return pl.BlockSpec((rows, columns), lambda f, o: (0, 0), pipeline_mode=pl.Buffered(1))

    part = pl.BlockSpec((deep, width), lambda f, o: (0, f))
    out = pl.pallas_call(
        functools.partial(expert_kernel, n),
        grid_spec=pltpu.PrefetchScalarGridSpec(
            num_scalar_prefetch=1,
            grid=(hidden // width,),
            in_specs=[full(model), full(model), full(1)] + [part] * n,
            out_specs=[full(model), full(model), full(1)] + [part] * n,
        ),
        out_shape=[jax.ShapeDtypeStruct((rows, model), f32)] * 2
        + [jax.ShapeDtypeStruct((rows, 1), f32)]
        + [jax.ShapeDtypeStruct((deep, hidden), bf16)] * n,
        compiler_params=pltpu.CompilerParams(vmem_limit_bytes=56 << 20),
    )(owner, x, g, mix, *weights)
    return out[0], out[1], out[2], out[3:]


def inverse_rms(values):
    return lax.rsqrt(jnp.mean(values * values, axis=-1, keepdims=True) + epsilon)


def norm_back(values, inverse, gain_vector, grad_rows):
    scaled = values * inverse
    weighted = grad_rows * gain_vector
    return inverse * (weighted - scaled * jnp.mean(weighted * scaled, axis=-1, keepdims=True))


def rotate(values, cosine, sine):
    half_dim = values.shape[-1] // 2
    first, second = values[..., :half_dim], values[..., half_dim:]
    return jnp.concatenate([first * cosine - second * sine, second * cosine + first * sine], axis=-1)


def by_head(rows, heads):
    return rows.reshape(rows.shape[0], heads, HEAD_DIM).transpose(1, 0, 2)


def by_row(heads):
    return heads.transpose(1, 0, 2).reshape(heads.shape[1], -1)


def local(
    tokens,
    segment_ids,
    routes,
    attn_gain,
    query_weight,
    key_weight,
    value_weight,
    out_weight,
    query_gain,
    key_gain,
    ffn_gain,
    router_weight,
    gate_weight,
    up_weight,
    down_weight,
    d_output,
):
    rows, model = tokens.shape
    owners, shards = lax.axis_size("expert"), lax.axis_size("wshard")
    rank = lax.axis_index("expert")
    local_experts = gate_weight.shape[0]
    experts = local_experts * owners
    heads = HEADS // shards
    wide = heads * HEAD_DIM
    root_dim = math.sqrt(HEAD_DIM)
    ring = Ring("wshard")
    rel = relative(owners)

    token_blocks = ring.gather(tokens)
    quarter = query_weight.shape[0] // owners
    own_rows = jnp.stack(
        [
            lax.dynamic_slice_in_dim(w, rank * quarter, quarter).reshape(quarter, shards, wide)
            for w in (query_weight, key_weight, value_weight)
        ],
        axis=2,
    )
    own_columns = lax.all_to_all(
        own_rows.transpose(1, 0, 2, 3), "wshard", split_axis=0, concat_axis=0, tiled=True
    )
    qkv_weight = (
        gather_bits(own_columns.reshape(shards, quarter, 3 * wide), "expert")
        .transpose(1, 0, 2, 3)
        .reshape(model, 3 * wide)
    )
    named = jnp.sum(
        (routes[:, :, None] == jnp.arange(experts, dtype=jnp.int32)).astype(f32), axis=1
    )
    named_all = jnp.concatenate(gather_relative(named, "expert"), axis=0)
    grad_all = jnp.concatenate(gather_relative(d_output, "expert"), axis=0)
    packed = [
        jnp.concatenate([gate_weight[i], up_weight[i], down_weight[i].T], axis=0)
        for i in range(local_experts)
    ]
    expert_weights = [ring.gather(packed[i], far_up=i % 2 == 1) for i in range(local_experts)]

    stream_all = jnp.concatenate(token_blocks, axis=0).astype(f32)
    inverse_all = inverse_rms(stream_all)
    normed_all = (stream_all * inverse_all * attn_gain).astype(bf16)
    sequence = rows * shards
    position = (ring.owner[:, None] * rows + jnp.arange(rows, dtype=jnp.int32)).reshape(-1)
    frequency = rope_base ** (
        -2.0 * jnp.arange(HEAD_DIM // 2, dtype=f32) / HEAD_DIM
    )
    angles = position.astype(f32)[:, None] * frequency[None, :]
    cosine, sine = jnp.cos(angles), jnp.sin(angles)
    segments = segment_ids.reshape(shards, rows)[ring.owner].reshape(-1)
    same = (segments[:, None] == segments[None, :])[None]

    raw = mm(normed_all, qkv_weight)
    query_raw = by_head(raw[:, :wide], heads)
    key_raw = by_head(raw[:, wide : 2 * wide], heads)
    values = by_head(raw[:, 2 * wide :].astype(bf16), heads)
    query_inverse, key_inverse = inverse_rms(query_raw), inverse_rms(key_raw)
    queries = rotate(query_raw * query_inverse * query_gain, cosine, sine).astype(bf16)
    keys = rotate(key_raw * key_inverse * key_gain, cosine, sine).astype(bf16)
    scores = jnp.einsum("hqd,hkd->hqk", queries, keys, preferred_element_type=f32) / root_dim
    scores = jnp.where(same, scores, -1e30)
    exponent = jnp.exp(scores - jnp.max(scores, axis=-1, keepdims=True))
    probs = exponent / jnp.sum(exponent, axis=-1, keepdims=True)
    probs_low = probs.astype(bf16)
    mixed = by_row(
        jnp.einsum("hqk,hkd->hqd", probs_low, values, preferred_element_type=f32).astype(bf16)
    )
    attended_part = mm(mixed, out_weight).astype(bf16).reshape(shards, rows, model)
    attended = ring.scatter([attended_part[j] for j in range(shards)])

    stream = tokens.astype(f32)
    middle = stream + attended
    ffn_inverse = inverse_rms(middle)
    ffn_low = (middle * ffn_inverse * ffn_gain).astype(bf16)

    ffn_all = jnp.concatenate(gather_relative(ffn_low, "expert"), axis=0)
    logits = mm(ffn_all, router_weight)
    logits = jnp.where(named_all > 0, logits, -jnp.inf)
    lifted = jnp.exp(logits - jnp.max(logits, axis=1, keepdims=True))
    mixing = lifted / jnp.sum(lifted, axis=1, keepdims=True)
    which = jnp.arange(experts, dtype=jnp.int32)[None, :]
    produced = row_grads = None
    mixing_grads = []
    weight_parts = []
    for i in range(local_experts):
        mix = jnp.sum(
            jnp.where(which == rank * local_experts + i, mixing, 0.0), axis=1, keepdims=True
        )
        y, dx, mg, parts = expert_pass(ring.owner, ffn_all, grad_all, mix, expert_weights[i])
        produced = y if i == 0 else produced + y
        row_grads = dx if i == 0 else row_grads + dx
        mixing_grads.append(mg)
        weight_parts.append(parts)

    def split(values):
        return [values[j * rows : (j + 1) * rows] for j in range(owners)]

    ffn_grad = scatter_relative(split(row_grads), "expert")
    expert_out = scatter_relative(split(produced), "expert")
    mixing_own = mixing[:rows]
    mixing_grad = jnp.zeros_like(mixing_own)
    for r, block in zip(rel, split(jnp.concatenate(mixing_grads, axis=1))):
        came = block
        if r:
            came = lax.ppermute(block, "expert", [(i, i ^ r) for i in range(owners)])
        for i in range(local_experts):
            at = which == (rank ^ r) * local_experts + i
            mixing_grad = jnp.where(at, came[:, i : i + 1], mixing_grad)

    final_stream = middle + expert_out
    output = final_stream.astype(bf16)
    logits_grad = mixing_own * (
        mixing_grad - jnp.sum(mixing_own * mixing_grad, axis=1, keepdims=True)
    )
    router_grad = lax.dot_general(
        logits_grad, ffn_low.astype(f32), TN, precision=highest, preferred_element_type=f32
    )
    ffn_grad = ffn_grad + lax.dot_general(
        logits_grad, router_weight.astype(f32), NT, precision=highest, preferred_element_type=f32
    )
    ffn_gain_grad = jnp.sum(ffn_grad * (middle * ffn_inverse), axis=0)
    middle_grad = d_output.astype(f32) + norm_back(middle, ffn_inverse, ffn_gain, ffn_grad)
    attended_low = middle_grad.astype(bf16)

    attended_all = jnp.concatenate(ring.gather(attended_low), axis=0)
    mixed_grad = by_head(mm(attended_all, out_weight, NT).astype(bf16), heads)
    out_grad = mm(mixed, attended_all, TN)
    probs_grad = jnp.einsum("hqd,hkd->hqk", mixed_grad, values, preferred_element_type=f32)
    scores_grad = (
        probs * (probs_grad - jnp.sum(probs * probs_grad, axis=-1, keepdims=True))
    ).astype(bf16)
    query_rot = jnp.einsum("hqk,hkd->hqd", scores_grad, keys, preferred_element_type=f32) / root_dim
    key_rot = jnp.einsum("hqk,hqd->hkd", scores_grad, queries, preferred_element_type=f32) / root_dim
    value_grad = jnp.einsum(
        "hqk,hqd->hkd", probs_low, mixed_grad, preferred_element_type=f32
    ).astype(bf16)
    query_grad = rotate(query_rot, cosine, -sine)
    key_grad = rotate(key_rot, cosine, -sine)
    query_gain_grad = jnp.sum(query_grad * (query_raw * query_inverse), axis=(0, 1))
    key_gain_grad = jnp.sum(key_grad * (key_raw * key_inverse), axis=(0, 1))
    query_low = norm_back(query_raw, query_inverse, query_gain, query_grad).astype(bf16)
    key_low = norm_back(key_raw, key_inverse, key_gain, key_grad).astype(bf16)
    raw_grad = jnp.concatenate([by_row(query_low), by_row(key_low), by_row(value_grad)], axis=1)

    normed_part = mm(raw_grad, qkv_weight, NT)
    attn_gain_grad = jnp.sum(normed_part * (stream_all * inverse_all), axis=0)
    normed_part = normed_part.astype(bf16).reshape(shards, rows, model)
    normed_grad = ring.scatter([normed_part[j] for j in range(shards)])
    tokens_grad = (
        middle_grad + norm_back(stream, inverse_all[:rows], attn_gain, normed_grad)
    ).astype(bf16)

    qkv_grad = mm(normed_all, raw_grad, TN).astype(bf16)
    qkv_grad = qkv_grad.reshape(shards, owners, quarter, 3 * wide).transpose(1, 0, 2, 3)
    qkv_grad = scatter_bits(qkv_grad, "expert")
    qkv_grad = lax.all_to_all(qkv_grad, "wshard", split_axis=0, concat_axis=0, tiled=True)
    qkv_grad = gather_bits(qkv_grad, "expert").reshape(owners, shards, quarter, 3, wide)
    qkv_grad = qkv_grad.transpose(3, 0, 2, 1, 4).reshape(3, owners * quarter, model).astype(f32)
    out_grad = out_grad.astype(bf16).reshape(owners, -1, model)
    out_grad = gather_bits(scatter_bits(out_grad, "expert"), "expert")
    out_grad = out_grad.reshape(-1, model).astype(f32)
    summed = [ring.scatter(weight_parts[i], far_up=i % 2 == 1) for i in range(local_experts)]
    depth = gate_weight.shape[1]
    gate_weight_grad = jnp.stack([s[:depth] for s in summed])
    up_weight_grad = jnp.stack([s[depth : 2 * depth] for s in summed])
    down_weight_grad = jnp.stack([s[2 * depth :].T for s in summed])

    squares = jnp.stack(
        [
            jnp.sum(middle * middle),
            jnp.sum(final_stream * final_stream),
            jnp.sum(attended * attended),
            jnp.sum(expert_out * expert_out),
        ]
    )
    early = jnp.concatenate([router_grad.reshape(-1), ffn_gain_grad, jnp.pad(squares, (0, 124))])
    early = sum_all(early.reshape(-1, 128)).reshape(-1)
    late = jnp.concatenate([attn_gain_grad, query_gain_grad, key_gain_grad])
    late = sum_all(late.reshape(-1, 128)).reshape(-1)
    router_size = experts * model
    router_weight_grad = early[:router_size].reshape(experts, model).T
    ffn_gain_grad = early[router_size : router_size + model]
    stream_rms = jnp.sqrt(
        early[router_size + model : router_size + model + 4] / (rows * owners * shards * model)
    )
    return (
        output,
        tokens_grad,
        late[:model],
        qkv_grad[0],
        qkv_grad[1],
        qkv_grad[2],
        out_grad,
        late[model : model + HEAD_DIM],
        late[model + HEAD_DIM :],
        ffn_gain_grad,
        router_weight_grad,
        gate_weight_grad,
        up_weight_grad,
        down_weight_grad,
        stream_rms,
    )


def solution(mesh):
    rows = P(("expert", "wshard"), None)
    shard = P("wshard", None)
    wide = P("expert", "wshard", None)
    tall = P("expert", None, "wshard")
    return jax.shard_map(
        local,
        mesh=mesh,
        in_specs=(rows, P("expert"), rows, P(), shard, shard, shard, shard)
        + (P(), P(), P(), P(), wide, wide, tall, rows),
        out_specs=(rows, rows, P(), shard, shard, shard, shard)
        + (P(), P(), P(), P(), wide, wide, tall, P()),
        check_vma=False,
    )
```

```python
import functools
import math

import jax
import jax.numpy as jnp
from jax import lax
from jax.experimental import pallas as pl
from jax.experimental.pallas import tpu as pltpu
from jax.sharding import PartitionSpec as P

HEADS = 16
HEAD_DIM = 128
epsilon = 1e-06
rope_base = 50000.0
highest = lax.Precision.HIGHEST
bf16 = jnp.bfloat16
f32 = jnp.float32

NN = (((1,), (0,)), ((), ()))
NT = (((1,), (1,)), ((), ()))
TN = (((0,), (0,)), ((), ()))


def mm(a, b, dims=NN):
    return lax.dot_general(a, b, dims, preferred_element_type=f32)


def tie(*arrays):
    return lax.optimization_barrier(arrays)


def after(x, *others):
    return lax.optimization_barrier((x, others))[0]


def ring_order(n):
    return list(range(0, n, 2)) + list(range(n - 1, 0, -2))


class Ring:
    def __init__(self, axis, groups=1):
        self.axis = axis
        total = lax.axis_size(axis)
        n = total // groups
        order = ring_order(n)
        self.down = [
            (g * n + order[i], g * n + order[(i + 1) % n]) for g in range(groups) for i in range(n)
        ]
        self.up = [(b, a) for a, b in self.down]
        place = [order.index(w % n) for w in range(total)]
        here = jnp.asarray(place, jnp.int32)[lax.axis_index(axis)]
        self.half = n // 2
        self.offsets = [0]
        for s in range(1, self.half):
            self.offsets += [-s, s]
        self.offsets.append(-self.half)
        table = jnp.asarray(order, jnp.int32)
        first = lax.axis_index(axis) // n * n
        self.owner = first + table[(here + jnp.asarray(self.offsets, jnp.int32) + n) % n]

    def hop(self, moving):
        return {
            sign: lax.ppermute(block, self.axis, self.down if sign == 1 else self.up)
            for sign, block in moving.items()
        }

    def gather(self, own, halves=False, hook=None):
        got = {0: own}
        moving = {1: own, -1: own}
        for s in range(1, self.half + 1):
            if s == self.half:
                if halves:
                    middle = own.shape[0] // 2
                    moving = {1: moving[1][:middle], -1: moving[-1][middle:]}
                else:
                    moving.pop(-1)
            if hook:
                moving = hook(s, moving)
            moving = self.hop(moving)
            for sign, block in moving.items():
                got[-s * sign] = block
        blocks = [got[o] for o in self.offsets]
        return blocks + [moving[-1]] if halves else blocks

    def begin(self, parts, halves=False):
        moving = {1: parts[2 * self.half - 1]}
        if halves:
            moving[-1] = parts[-1]
        return self.hop(moving)

    def scatter(self, parts, halves=False, hook=None):
        return self.finish(parts, self.begin(parts, halves), halves, hook)

    def finish(self, parts, moving, halves=False, hook=None):
        part = dict(zip(self.offsets, parts))
        moving = dict(moving)
        for s in range(2, self.half + 1):
            distance = self.half - s + 1
            for sign in (1, -1):
                own = part[sign * distance]
                if sign not in moving:
                    moving[sign] = own
                elif moving[sign].shape == own.shape:
                    moving[sign] = (moving[sign].astype(f32) + own.astype(f32)).astype(bf16)
                else:
                    middle = own.shape[0] // 2
                    low, high = own[:middle], own[middle:]
                    if sign == 1:
                        low = (moving[sign].astype(f32) + low.astype(f32)).astype(bf16)
                    else:
                        high = (moving[sign].astype(f32) + high.astype(f32)).astype(bf16)
                    moving[sign] = jnp.concatenate([low, high], axis=0)
            if hook:
                moving = hook(s, moving)
            moving = self.hop(moving)
        if hook:
            moving = hook(self.half + 1, moving)
        total = part[0].astype(f32)
        for block in moving.values():
            total = total + block.astype(f32)
        return total


def bits_of(size):
    return [1 << b for b in range(size.bit_length() - 1)]


def swap(x, axis, bit):
    return lax.ppermute(x, axis, [(i, i ^ bit) for i in range(lax.axis_size(axis))])


def gather_bits(x, axis, holds=()):
    index = lax.axis_index(axis)
    out = x[None]
    for k, bit in enumerate(reversed(bits_of(lax.axis_size(axis)))):
        came = swap(out, axis, bit)
        if k < len(holds):
            came = after(came, holds[k])
        high = (index & bit) != 0
        out = jnp.stack([jnp.where(high, came, out), jnp.where(high, out, came)], axis=1)
        out = out.reshape((-1,) + x.shape)
    return out


def scatter_bits(x, axis):
    index = lax.axis_index(axis)
    for bit in bits_of(lax.axis_size(axis)):
        pairs = x.reshape((-1, 2) + x.shape[1:])
        high = (index & bit) != 0
        keep = jnp.where(high, pairs[:, 1], pairs[:, 0])
        came = swap(jnp.where(high, pairs[:, 0], pairs[:, 1]), axis, bit)
        x = (keep.astype(f32) + came.astype(f32)).astype(bf16)
    return x[0]


class Sum:
    def __init__(self, x):
        self.total = x
        self.left = [
            (axis, bit) for axis in ("expert", "wshard") for bit in bits_of(lax.axis_size(axis))
        ]

    def step(self):
        if self.left:
            self.total = self.total + swap(self.total, *self.left.pop(0))
        return self.total

    def finish(self):
        while self.left:
            self.step()
        return self.total


class Group:
    def __init__(self, split):
        self.owners = lax.axis_size("expert")
        self.split = split
        self.far = lax.axis_size("wshard") // 2
        self.rel = [0]
        for bit in reversed(bits_of(self.owners)):
            self.rel += [r ^ bit for r in self.rel]

    def far_block(self, x):
        return [swap(x, "wshard", self.far)] if self.split == 2 else []

    def join(self, own, far):
        if far:
            own = [block for pair in zip(own, far) for block in pair]
        return jnp.concatenate(own, axis=0)

    def gather(self, x, hook=None):
        blocks = [x]
        for bit in reversed(bits_of(self.owners)):
            came = [swap(b, "expert", bit) for b in blocks]
            if hook:
                came = hook(came)
            blocks += came
        return blocks

    def scatter(self, x):
        for bit in bits_of(self.owners):
            half = x.shape[0] // 2
            send = x[half:].astype(bf16)
            x = x[:half] + swap(send, "expert", bit).astype(f32)
        return x

    def exchange(self, x):
        x = x.reshape((self.owners, self.split, -1) + x.shape[1:])
        own = x[:, 0]
        if self.split == 2:
            own = own + swap(x[:, 1], "wshard", self.far)
        return [
            lax.ppermute(own[k], "expert", [(i, i ^ r) for i in range(self.owners)]) if r else own[k]
            for k, r in enumerate(self.rel)
        ]


def expert_kernel(n, depth, width, sums, owner, x_ref, g_ref, m_ref, *refs):
    weights, refs = refs[:n], refs[n:]
    before, refs = refs[:sums], refs[sums:]
    (y_ref, dx_ref, mg_ref), refs = refs[:3], refs[3:]
    grads, refs = refs[:n], refs[n:]
    w_buf, d_buf, mixed_ref, gate_ref, up_ref, w_sem, d_sem, s_sem = refs
    step, steps = pl.program_id(0), pl.num_programs(0)
    slot = step % 2
    starts = [sum(w.shape[0] for w in weights[:j]) for j in range(n)]

    def columns(at):
        return pl.ds(pl.multiple_of(at * width, width), width)

    def rows_of(j):
        return pl.ds(starts[j], weights[j].shape[0])

    def get(at, j):
        return pltpu.make_async_copy(
            weights[j].at[:, columns(at)], w_buf.at[at % 2, rows_of(j)], w_sem.at[at % 2, j]
        )

    def put(at, j):
        return pltpu.make_async_copy(
            d_buf.at[at % 2, rows_of(j)], grads[j].at[:, columns(at)], d_sem.at[at % 2, j]
        )

    def resume(k):
        return pltpu.make_async_copy(before[k], (y_ref, dx_ref)[k], s_sem.at[k])

    @pl.when(step == 0)
    def _():
        for j in range(n):
            get(step, j).start()
        for k in range(sums):
            resume(k).start()
        if not sums:
            y_ref[...] = jnp.zeros_like(y_ref)
            dx_ref[...] = jnp.zeros_like(dx_ref)
        mg_ref[...] = jnp.zeros_like(mg_ref)

    @pl.when(step + 1 < steps)
    def _():
        for j in range(n):
            get(step + 1, j).start()

    for j in range(n):
        get(step, j).wait()

    @pl.when(step >= 2)
    def _():
        for j in range(n):
            put(step - 2, j).wait()

    places = []
    for j in range(w_buf.shape[1] // (3 * depth)):
        at = pl.ds(pl.multiple_of(owner[j] * depth, depth), depth)
        places.append((at, [pl.ds((3 * j + part) * depth, depth) for part in range(3)]))
    count = x_ref.shape[0]
    tile = min(count, 512)
    for start in range(0, count, tile):
        here = pl.ds(start, tile)
        gate = up = back = None
        for at, rows in places:
            x, g = x_ref[here, at], g_ref[here, at]
            a, b, c = (
                mm(x, w_buf[slot, rows[0]]),
                mm(x, w_buf[slot, rows[1]]),
                mm(g, w_buf[slot, rows[2]]),
            )
            gate, up, back = (a, b, c) if gate is None else (gate + a, up + b, back + c)
        sig = 1.0 / (1.0 + jnp.exp(-gate))
        act = gate * sig
        hidden = act * up
        mix = m_ref[here]
        mg_ref[here] += jnp.sum(hidden * back, axis=1, keepdims=True)
        mixed_ref[here] = (mix * hidden).astype(bf16)
        hidden_grad = mix * back
        gate_ref[here] = (hidden_grad * up * sig * (1.0 + gate * (1.0 - sig))).astype(bf16)
        up_ref[here] = (hidden_grad * act).astype(bf16)

    if sums:

        @pl.when(step == 0)
        def _():
            for k in range(sums):
                resume(k).wait()

    mixed, gate_grad, up_grad = mixed_ref[...], gate_ref[...], up_ref[...]
    for at, rows in places:
        x, g = x_ref[:, at], g_ref[:, at]
        y_ref[:, at] += mm(mixed, w_buf[slot, rows[2]], NT)
        dx_ref[:, at] += mm(gate_grad, w_buf[slot, rows[0]], NT) + mm(
            up_grad, w_buf[slot, rows[1]], NT
        )
        d_buf[slot, rows[0]] = mm(x, gate_grad, TN).astype(bf16)
        d_buf[slot, rows[1]] = mm(x, up_grad, TN).astype(bf16)
        d_buf[slot, rows[2]] = mm(g, mixed, TN).astype(bf16)
    for j in range(n):
        put(step, j).start()

    @pl.when(step == steps - 1)
    def _():
        for j in range(n):
            put(step - 1, j).wait()
            put(step, j).wait()


def expert_pass(owner, x, g, mix, weights, sums, width):
    n = len(weights)
    rows, model = x.shape
    deep, hidden = sum(w.shape[0] for w in weights), weights[0].shape[1]

    def full(columns):
        return pl.BlockSpec((rows, columns), lambda f, o: (0, 0), pipeline_mode=pl.Buffered(1))

    anywhere = pl.BlockSpec(memory_space=pl.ANY)
    out = pl.pallas_call(
        functools.partial(expert_kernel, n, model // owner.shape[0], width, len(sums)),
        grid_spec=pltpu.PrefetchScalarGridSpec(
            num_scalar_prefetch=1,
            grid=(hidden // width,),
            in_specs=[full(model), full(g.shape[1]), full(1)] + [anywhere] * (n + len(sums)),
            out_specs=[full(model), full(model), full(1)] + [anywhere] * n,
            scratch_shapes=[
                pltpu.VMEM((2, deep, width), bf16),
                pltpu.VMEM((2, deep, width), bf16),
                pltpu.VMEM((rows, width), bf16),
                pltpu.VMEM((rows, width), bf16),
                pltpu.VMEM((rows, width), bf16),
                pltpu.SemaphoreType.DMA((2, n)),
                pltpu.SemaphoreType.DMA((2, n)),
                pltpu.SemaphoreType.DMA((2,)),
            ],
        ),
        out_shape=[jax.ShapeDtypeStruct((rows, model), f32)] * 2
        + [jax.ShapeDtypeStruct((rows, 1), f32)]
        + [jax.ShapeDtypeStruct(w.shape, bf16) for w in weights],
        compiler_params=pltpu.CompilerParams(vmem_limit_bytes=60 << 20),
        cost_estimate=pl.CostEstimate(
            flops=18 * rows * model * hidden, transcendentals=0, bytes_accessed=4 * deep * hidden
        ),
    )(owner, x, g, mix, *weights, *sums)
    return list(out[:2]), out[2], list(out[3:])


def inverse_rms(values):
    return lax.rsqrt(jnp.mean(values * values, axis=-1, keepdims=True) + epsilon)


def norm_back(values, inverse, gain_vector, grad_rows):
    scaled = values * inverse
    weighted = grad_rows * gain_vector
    return inverse * (weighted - scaled * jnp.mean(weighted * scaled, axis=-1, keepdims=True))


def rotate(values, cosine, sine):
    return values * cosine + pltpu.roll(values, HEAD_DIM // 2, 1) * sine


def each_block(count, size, body):
    def one(k, carry):
        body(pl.ds(pl.multiple_of(k * size, size), size))
        return carry

    lax.fori_loop(0, count // size, one, 0)


def head_columns(h, part=0, heads=1):
    return pl.ds((part * heads + h) * HEAD_DIM, HEAD_DIM)


def scores_of(low_ref, seg_ref, segs_ref, here, h, heads):
    keys = low_ref[:, head_columns(h, 1, heads)]
    scores = mm(low_ref[here, head_columns(h)], keys, NT) * (1.0 / math.sqrt(HEAD_DIM))
    return jnp.where(seg_ref[here] == segs_ref[...], scores, -1e30)


def attention_kernel(n, heads, block, *refs):
    tokens, refs = refs[:n], refs[n:]
    w_ref, out_ref, gain_ref, qg_ref, kg_ref, cos_ref, sin_ref, seg_ref, segs_ref = refs[:9]
    normed_ref, inverse_ref, raw_ref, low_ref, lse_ref, mixed_ref = refs[9:15]
    parts = refs[15:]
    rows = tokens[0].shape[0]
    wide = heads * HEAD_DIM
    for b in range(n):
        here = pl.ds(b * rows, rows)
        x = tokens[b][...].astype(f32)
        inverse = inverse_rms(x)
        inverse_ref[here] = inverse
        normed_ref[here] = (x * inverse * gain_ref[...]).astype(bf16)

    def project(here):
        raw = mm(normed_ref[here], w_ref[...])
        raw_ref[here] = raw[:, : 2 * wide]
        low_ref[here, 2 * wide :] = raw[:, 2 * wide :].astype(bf16)
        for part, g_ref in ((0, qg_ref), (1, kg_ref)):
            for h in range(heads):
                at = (part * heads + h) * HEAD_DIM
                u = raw[:, at : at + HEAD_DIM]
                u = u * inverse_rms(u) * g_ref[...]
                low_ref[here, at : at + HEAD_DIM] = rotate(u, cos_ref[here], sin_ref[here]).astype(bf16)

    count = normed_ref.shape[0]
    each_block(count, block, project)

    def attend(here):
        for h in range(heads):
            scores = scores_of(low_ref, seg_ref, segs_ref, here, h, heads)
            top = jnp.max(scores, axis=-1, keepdims=True)
            lifted = jnp.exp(scores - top)
            total = jnp.sum(lifted, axis=-1, keepdims=True)
            probs = (lifted * (1.0 / total)).astype(bf16)
            lse_ref[here, h : h + 1] = top + jnp.log(total)
            mixed_ref[here, head_columns(h)] = mm(
                probs, low_ref[:, head_columns(h, 2, heads)]
            ).astype(bf16)

    each_block(count, block, attend)
    for b in range(n):
        parts[b][...] = mm(mixed_ref[pl.ds(b * rows, rows)], out_ref[...]).astype(bf16)


def attention_back_kernel(n, heads, block, *refs):
    grads, tokens, refs = refs[:n], refs[n : 2 * n], refs[2 * n :]
    w_ref, out_ref, qg_ref, kg_ref, cos_ref, sin_ref, seg_ref, segs_ref = refs[:8]
    inverse_ref, raw_ref, low_ref, lse_ref = refs[8:12]
    raw_grad_ref, gain_ref, head_gain_ref = refs[12:15]
    parts, refs = refs[15 : 15 + n], refs[15 + n :]
    mixed_ref, query_ref, key_ref, value_ref = refs
    rows = tokens[0].shape[0]
    wide = heads * HEAD_DIM
    scale = 1.0 / math.sqrt(HEAD_DIM)
    for b in range(n):
        mixed_ref[pl.ds(b * rows, rows)] = mm(grads[b][...], out_ref[...], NT).astype(bf16)
    key_ref[...] = jnp.zeros_like(key_ref)
    value_ref[...] = jnp.zeros_like(value_ref)

    def attend(here):
        for h in range(heads):
            at = head_columns(h)
            scores = scores_of(low_ref, seg_ref, segs_ref, here, h, heads)
            probs = jnp.exp(scores - lse_ref[here, h : h + 1])
            mixed_grad = mixed_ref[here, at]
            probs_grad = mm(mixed_grad, low_ref[:, head_columns(h, 2, heads)], NT)
            mean = jnp.sum(probs * probs_grad, axis=-1, keepdims=True)
            scores_grad = (probs * (probs_grad - mean)).astype(bf16)
            query_ref[here, at] = mm(scores_grad, low_ref[:, head_columns(h, 1, heads)]) * scale
            key_ref[:, at] += mm(scores_grad, low_ref[here, at], TN) * scale
            value_ref[:, at] += mm(probs.astype(bf16), mixed_grad, TN)

    count = mixed_ref.shape[0]
    each_block(count, block, attend)
    head_gain_ref[...] = jnp.zeros_like(head_gain_ref)

    def norms_back(here):
        raw_grad_ref[here, 2 * wide :] = value_ref[here].astype(bf16)
        for part, g_ref, rot_ref in ((0, qg_ref, query_ref), (1, kg_ref, key_ref)):
            for h in range(heads):
                at = (part * heads + h) * HEAD_DIM
                grad = rotate(rot_ref[here, head_columns(h)], cos_ref[here], -sin_ref[here])
                u = raw_ref[here, at : at + HEAD_DIM]
                inverse = inverse_rms(u)
                head_gain_ref[part : part + 1] += jnp.sum(
                    grad * (u * inverse), axis=0, keepdims=True
                )
                raw_grad_ref[here, at : at + HEAD_DIM] = norm_back(
                    u, inverse, g_ref[...], grad
                ).astype(bf16)

    each_block(count, block, norms_back)
    gain = None
    for b in range(n):
        here = pl.ds(b * rows, rows)
        part = mm(raw_grad_ref[here], w_ref[...], NT)
        parts[b][...] = part.astype(bf16)
        scaled = tokens[b][...].astype(f32) * inverse_ref[here]
        one = jnp.sum(part * scaled, axis=0, keepdims=True)
        gain = one if gain is None else gain + one
    gain_ref[...] = gain


def in_vmem(kernel, shapes, arrays, flops, scratch=()):
    return pl.pallas_call(
        kernel,
        in_specs=[pl.BlockSpec(memory_space=pltpu.VMEM)] * len(arrays),
        out_specs=[pl.BlockSpec(memory_space=pltpu.VMEM)] * len(shapes),
        out_shape=[jax.ShapeDtypeStruct(*shape) for shape in shapes],
        scratch_shapes=list(scratch),
        compiler_params=pltpu.CompilerParams(vmem_limit_bytes=60 << 20),
        cost_estimate=pl.CostEstimate(
            flops=flops,
            transcendentals=0,
            bytes_accessed=sum(a.size * a.dtype.itemsize for a in arrays),
        ),
    )(*arrays)


def local(
    tokens,
    segment_ids,
    routes,
    attn_gain,
    query_weight,
    key_weight,
    value_weight,
    out_weight,
    query_gain,
    key_gain,
    ffn_gain,
    router_weight,
    gate_weight,
    up_weight,
    down_weight,
    d_output,
):
    rows, model = tokens.shape
    owners, shards = lax.axis_size("expert"), lax.axis_size("wshard")
    rank = lax.axis_index("expert")
    local_experts = gate_weight.shape[0]
    experts = local_experts * owners
    heads = HEADS // shards
    wide = heads * HEAD_DIM
    ring = Ring("wshard")
    split = 2 if rows * owners <= 512 else 1
    far = shards // split
    group = Group(split)
    weight_ring = Ring("wshard", split)
    upper = lax.axis_index("wshard") >= far

    held = {}
    quarter = query_weight.shape[0] // owners
    own_rows = jnp.concatenate(
        [
            lax.dynamic_slice_in_dim(w, rank * quarter, quarter)
            .reshape(quarter, shards, wide)
            .transpose(1, 0, 2)
            for w in (query_weight, key_weight, value_weight)
        ],
        axis=2,
    )
    own_columns = lax.all_to_all(own_rows, "wshard", split_axis=0, concat_axis=0, tiled=True)
    named = jnp.sum(
        (routes[:, :, None] == jnp.arange(128, dtype=jnp.int32)).astype(bf16), axis=1
    )
    grad_rows = jnp.concatenate([d_output, named], axis=1)
    grad_far = group.far_block(grad_rows)

    def token_hook(s, moving):
        if s == 3:
            moving, held["columns"], held["grad"] = tie(moving, own_columns, grad_far)
            held["two"] = moving
        if s == ring.half:
            held["last"] = moving
        return moving

    token_blocks = ring.gather(tokens, hook=token_hook)
    qkv_weight = gather_bits(held["columns"], "expert", [held["last"]])
    qkv_weight = qkv_weight.transpose(1, 0, 2, 3).reshape(model, 3 * wide)
    grad_own = group.gather(after(grad_rows, held["two"]))
    grad_far = [b for block in held["grad"] for b in group.gather(block)]

    weights, _ = tie((gate_weight, up_weight, down_weight), held["two"])
    packed = [
        jnp.concatenate([weights[0][i], weights[1][i], weights[2][i].T], axis=0)
        for i in range(local_experts)
    ]
    half = packed[0].shape[1] // 2

    def cross(i, start):
        if split == 1:
            return packed[i][:0]
        send = jnp.where(upper, packed[i][:, :half], packed[i][:, half:])
        return swap(after(send, start), "wshard", far)

    def crossed(i, came):
        if split == 1:
            return packed[i]
        return jnp.concatenate(
            [jnp.where(upper, packed[i][:, half:], packed[i][:, :half]), came], axis=0
        )

    halves = split == 2
    block_owner = weight_ring.owner
    if split == 2:
        block_owner = jnp.stack([block_owner, block_owner ^ far], axis=1).reshape(-1)
    cross_first = cross(0, token_blocks[-1])

    sequence = rows * shards
    position = (ring.owner[:, None] * rows + jnp.arange(rows, dtype=jnp.int32)).reshape(-1)
    frequency = rope_base ** (-2.0 * jnp.arange(HEAD_DIM // 2, dtype=f32) / HEAD_DIM)
    angles = position.astype(f32)[:, None] * frequency[None, :]
    cosine, sine = jnp.cos(angles), jnp.sin(angles)
    tables = (
        jnp.concatenate([cosine, cosine], axis=1),
        jnp.concatenate([-sine, sine], axis=1),
    )
    segments = segment_ids.reshape(shards, rows)[ring.owner].reshape(-1)
    segments = (segments[:, None], segments[None, :])
    gains = (query_gain[None], key_gain[None])
    tile = 256
    normed_all, inverse_all, raw, low, log_total, mixed, *attended_part = in_vmem(
        functools.partial(attention_kernel, shards, heads, tile),
        [
            ((sequence, model), bf16),
            ((sequence, 1), f32),
            ((sequence, 2 * wide), f32),
            ((sequence, 3 * wide), bf16),
            ((sequence, heads), f32),
            ((sequence, wide), bf16),
        ]
        + [((rows, model), bf16)] * shards,
        [*token_blocks, qkv_weight, out_weight, attn_gain[None], *gains, *tables, *segments],
        2 * sequence * wide * (4 * model + 2 * sequence),
    )
    attended_part, cross_first, grad_own, grad_far = tie(
        attended_part, cross_first, grad_own, grad_far
    )
    first_block = crossed(0, cross_first)

    def attended_sum():
        part = dict(zip(ring.offsets, attended_part))
        moving = {1: part.pop(-ring.half)}
        for s in range(1, ring.half + 1):
            distance = ring.half - s + 1
            if distance < ring.half:
                for sign in (1, -1):
                    own = part[sign * distance]
                    if sign in moving:
                        own = (moving[sign].astype(f32) + own.astype(f32)).astype(bf16)
                    moving[sign] = own
            if s == 2:
                held["first"] = weight_ring.gather(after(first_block, moving), halves)
                held["second"] = cross(1, moving)
            if s == ring.half and weight_ring.half == 2:
                moving, near = tie(moving, held["first"][1:3])
                held["first"][1:3] = near
            moving = ring.hop(moving)
        total = part[0].astype(f32)
        for block in moving.values():
            total = total + block.astype(f32)
        return total

    attended = attended_sum()
    attended, cross_second = tie(attended, held["second"])

    stream = tokens.astype(f32)
    middle = stream + attended
    ffn_inverse = inverse_rms(middle)
    ffn_low = (middle * ffn_inverse * ffn_gain).astype(bf16)

    ffn_far = group.far_block(ffn_low)
    ffn_own = group.gather(ffn_low)
    second_block = crossed(1, after(cross_second, ffn_far or ffn_low))
    second_weights = weight_ring.gather(second_block, halves)
    ffn_far = [b for block in ffn_far for b in group.gather(block)]
    ffn_all = group.join(ffn_own, ffn_far)
    grad_and_names = group.join(grad_own, grad_far)
    first_weights = held["first"]
    near = 2 * weight_ring.half - 1
    ffn_all, first_weights, second_weights[:near] = tie(
        ffn_all, first_weights, second_weights[:near]
    )
    logits = mm(ffn_all, router_weight)
    logits = jnp.where(grad_and_names[:, model : model + experts] > 0, logits, -jnp.inf)
    lifted = jnp.exp(logits - jnp.max(logits, axis=1, keepdims=True))
    mixing = lifted / jnp.sum(lifted, axis=1, keepdims=True)
    which = jnp.arange(experts, dtype=jnp.int32)[None, :]
    mixes = [
        jnp.sum(jnp.where(which == rank * local_experts + i, mixing, 0.0), axis=1, keepdims=True)
        for i in range(local_experts)
    ]
    width = 256 if split == 2 else 128
    first_out = expert_pass(
        block_owner, ffn_all, grad_and_names, mixes[0], first_weights, [], width
    )
    first_out, second_weights[near:] = tie(first_out, second_weights[near:])
    sums, first_mixing, first_parts = first_out
    second_out = expert_pass(
        block_owner, ffn_all, grad_and_names, mixes[1], second_weights, sums, width
    )

    def first_hook(s, moving):
        if s == 2:
            held["h1"] = moving
        if s == weight_ring.half + 1:
            held["h2"] = moving
        return moving

    first_moving = weight_ring.begin(first_parts, halves)
    second_out, first_moving = tie(second_out, first_moving)
    (produced, row_grads), second_mixing, second_parts = second_out
    mixing_grads = [first_mixing, second_mixing]
    first_sum = weight_ring.finish(first_parts, first_moving, halves, hook=first_hook)
    came = group.exchange(jnp.concatenate(mixing_grads, axis=1))

    def far_sum(x, *hold):
        if split == 1:
            return x
        count = x.shape[0] // 2
        return x[:count] + swap(after(x[count:].astype(bf16), hold), "wshard", far).astype(f32)

    ffn_grad = far_sum(group.scatter(row_grads), held["h2"], came)
    mixing_own = mixing[:rows]
    mixing_grad = jnp.zeros_like(mixing_own)
    for r, block in zip(group.rel, came):
        for i in range(local_experts):
            at = which == (rank ^ r) * local_experts + i
            mixing_grad = jnp.where(at, block[:, i : i + 1], mixing_grad)

    logits_grad = mixing_own * (
        mixing_grad - jnp.sum(mixing_own * mixing_grad, axis=1, keepdims=True)
    )
    router_grad = lax.dot_general(
        logits_grad, ffn_low.astype(f32), TN, precision=highest, preferred_element_type=f32
    )
    ffn_grad = ffn_grad + lax.dot_general(
        logits_grad, router_weight.astype(f32), NT, precision=highest, preferred_element_type=f32
    )
    ffn_gain_grad = jnp.sum(ffn_grad * (middle * ffn_inverse), axis=0)
    middle_grad = d_output.astype(f32) + norm_back(middle, ffn_inverse, ffn_gain, ffn_grad)
    attended_low = middle_grad.astype(bf16)

    attended_blocks = ring.gather(attended_low)
    attended_all = attended_blocks[-1]
    produced = group.scatter(after(produced, attended_low))
    second_parts, first_sum, produced = after((second_parts, first_sum, produced), attended_all)

    def uncross(total):
        if split == 1:
            return total[:0]
        return swap(total[3 * depth :].astype(bf16), "wshard", far)

    def uncrossed(total, other):
        if split == 1:
            return total
        own, other = total[: 3 * depth], other.astype(f32)
        return jnp.concatenate(
            [jnp.where(upper, other, own), jnp.where(upper, own, other)], axis=1
        )

    depth = gate_weight.shape[1]
    first_home = uncross(first_sum)
    expert_part = produced[rows:] if split == 2 else produced[:0]
    expert_far = group.far_block(expert_part.astype(bf16))
    second_moving = weight_ring.begin(second_parts, halves)
    raw_grad, attn_gain_grad, head_gain_grad, *normed_part = in_vmem(
        functools.partial(attention_back_kernel, shards, heads, tile),
        [((sequence, 3 * wide), bf16), ((1, model), f32), ((2, HEAD_DIM), f32)]
        + [((rows, model), bf16)] * shards,
        [*attended_blocks, *token_blocks, qkv_weight, out_weight, *gains, *tables, *segments]
        + [inverse_all, raw, low, log_total],
        2 * sequence * wide * (4 * model + 5 * sequence),
        [pltpu.VMEM((sequence, wide), dtype) for dtype in (bf16, f32, f32, f32)],
    )
    normed_part, raw_grad, second_moving, first_home = tie(
        normed_part, raw_grad, second_moving, first_home
    )
    query_gain_grad, key_gain_grad = head_gain_grad[0], head_gain_grad[1]
    router_size = experts * model
    squares = jnp.stack([jnp.sum(middle * middle), jnp.sum(attended * attended)])
    small = Sum(
        jnp.concatenate(
            [
                router_grad.reshape(-1),
                ffn_gain_grad,
                attn_gain_grad[0],
                query_gain_grad,
                key_gain_grad,
                jnp.pad(squares, (0, 126)),
            ]
        ).reshape(-1, 128)
    )

    def normed_hook(s, moving):
        if 1 < s <= ring.half:
            moving, small.total = tie(moving, small.step())
        held["n%d" % s] = moving
        return moving

    normed_grad = ring.scatter(normed_part, hook=normed_hook)
    tokens_grad = (
        middle_grad + norm_back(stream, inverse_all[:rows], attn_gain, normed_grad)
    ).astype(bf16)

    qkv_grad = mm(normed_all, raw_grad, TN).astype(bf16)
    qkv_grad = qkv_grad.reshape(shards, owners, quarter, 3 * wide).transpose(1, 0, 2, 3)
    qkv_grad = scatter_bits(qkv_grad, "expert")
    qkv_grad = lax.all_to_all(qkv_grad, "wshard", split_axis=0, concat_axis=0, tiled=True)
    qkv_grad = gather_bits(qkv_grad, "expert")
    query_weight_grad, key_weight_grad, value_weight_grad = [
        qkv_grad[..., i * wide : (i + 1) * wide]
        .transpose(0, 2, 1, 3)
        .reshape(owners * quarter, model)
        .astype(f32)
        for i in range(3)
    ]
    out_grad = mm(mixed, after(jnp.concatenate(attended_blocks, axis=0), held["n2"]), TN)
    out_grad = out_grad.astype(bf16).reshape(owners, -1, model)
    out_grad = gather_bits(scatter_bits(out_grad, "expert"), "expert")
    out_grad = out_grad.reshape(-1, model).astype(f32)

    def second_hook(s, moving):
        if s == 2:
            moving = after(moving, held["n%d" % ring.half])
        return moving

    second_sum = weight_ring.finish(second_parts, second_moving, halves, hook=second_hook)
    expert_far = after(expert_far, normed_grad)
    summed = [uncrossed(first_sum, first_home), uncrossed(second_sum, uncross(second_sum))]
    expert_out = produced[:rows]
    for block in expert_far:
        expert_out = expert_out + block.astype(f32)
    final_stream = middle + expert_out
    output = final_stream.astype(bf16)
    gate_weight_grad = jnp.stack([s[:depth] for s in summed])
    up_weight_grad = jnp.stack([s[depth : 2 * depth] for s in summed])
    down_weight_grad = jnp.stack([s[2 * depth :].T for s in summed])

    total = small.finish().reshape(-1)
    squares = Sum(
        jnp.pad(
            jnp.stack([jnp.sum(final_stream * final_stream), jnp.sum(expert_out * expert_out)]),
            (0, 126),
        ).reshape(1, 128)
    ).finish()[0]
    sizes = [router_size, model, model, HEAD_DIM, HEAD_DIM, 2]
    starts = [sum(sizes[:k]) for k in range(len(sizes))]
    router_sum, ffn_gain_grad, attn_gain_grad, query_gain_grad, key_gain_grad, near_squares = [
        total[a : a + b] for a, b in zip(starts, sizes)
    ]
    router_weight_grad = router_sum.reshape(experts, model).T
    squares = jnp.stack([near_squares[0], squares[0], near_squares[1], squares[1]])
    stream_rms = jnp.sqrt(squares / (rows * owners * shards * model))
    return (
        output,
        tokens_grad,
        attn_gain_grad,
        query_weight_grad,
        key_weight_grad,
        value_weight_grad,
        out_grad,
        query_gain_grad,
        key_gain_grad,
        ffn_gain_grad,
        router_weight_grad,
        gate_weight_grad,
        up_weight_grad,
        down_weight_grad,
        stream_rms,
    )


def solution(mesh):
    rows = P(("expert", "wshard"), None)
    shard = P("wshard", None)
    wide = P("expert", "wshard", None)
    tall = P("expert", None, "wshard")
    return jax.shard_map(
        local,
        mesh=mesh,
        in_specs=(rows, P("expert"), rows, P(), shard, shard, shard, shard)
        + (P(), P(), P(), P(), wide, wide, tall, rows),
        out_specs=(rows, rows, P(), shard, shard, shard, shard)
        + (P(), P(), P(), P(), wide, wide, tall, P()),
        check_vma=False,
    )
```

```python
import functools
import math

import jax
import jax.numpy as jnp
from jax import lax
from jax.experimental import pallas as pl
from jax.experimental.pallas import tpu as pltpu
from jax.sharding import PartitionSpec as P

HEADS = 16
HEAD_DIM = 128
epsilon = 1e-06
rope_base = 50000.0
highest = lax.Precision.HIGHEST
bf16 = jnp.bfloat16
f32 = jnp.float32

NN = (((1,), (0,)), ((), ()))
NT = (((1,), (1,)), ((), ()))
TN = (((0,), (0,)), ((), ()))


def mm(a, b, dims=NN):
    return lax.dot_general(a, b, dims, preferred_element_type=f32)


def tie(*arrays):
    return lax.optimization_barrier(arrays)


def after(x, *others):
    return lax.optimization_barrier((x, others))[0]


def ring_order(n):
    return list(range(0, n, 2)) + list(range(n - 1, 0, -2))


class Ring:
    def __init__(self, axis, groups=1):
        self.axis = axis
        total = lax.axis_size(axis)
        n = total // groups
        order = ring_order(n)
        self.down = [
            (g * n + order[i], g * n + order[(i + 1) % n]) for g in range(groups) for i in range(n)
        ]
        self.up = [(b, a) for a, b in self.down]
        place = [order.index(w % n) for w in range(total)]
        here = jnp.asarray(place, jnp.int32)[lax.axis_index(axis)]
        self.half = n // 2
        self.offsets = [0]
        for s in range(1, self.half):
            self.offsets += [-s, s]
        self.offsets.append(-self.half)
        table = jnp.asarray(order, jnp.int32)
        first = lax.axis_index(axis) // n * n
        self.owner = first + table[(here + jnp.asarray(self.offsets, jnp.int32) + n) % n]

    def hop(self, moving):
        return {
            sign: lax.ppermute(block, self.axis, self.down if sign == 1 else self.up)
            for sign, block in moving.items()
        }

    def gather(self, own, halves=False, hook=None, first=None):
        got = {0: own}
        moving = {1: own, -1: own}
        for s in range(1, self.half + 1):
            if s == self.half:
                if halves:
                    middle = own.shape[0] // 2
                    moving = {1: moving[1][:middle], -1: moving[-1][middle:]}
                else:
                    moving.pop(-1)
            if hook:
                moving = hook(s, moving)
            moving = first if s == 1 and first else self.hop(moving)
            for sign, block in moving.items():
                got[-s * sign] = block
        blocks = [got[o] for o in self.offsets]
        return blocks + [moving[-1]] if halves else blocks

    def begin(self, parts, halves=False):
        moving = {1: parts[2 * self.half - 1]}
        if halves:
            moving[-1] = parts[-1]
        return self.hop(moving)

    def scatter(self, parts, halves=False, hook=None):
        return self.finish(parts, self.begin(parts, halves), halves, hook)

    def added(self, parts, moving, s):
        part = dict(zip(self.offsets, parts))
        distance = self.half - s + 1
        out = {}
        for sign in (1, -1):
            own = part[sign * distance]
            if sign not in moving:
                out[sign] = own
            elif moving[sign].shape == own.shape:
                out[sign] = (moving[sign].astype(f32) + own.astype(f32)).astype(bf16)
            else:
                middle = own.shape[0] // 2
                low, high = own[:middle], own[middle:]
                if sign == 1:
                    low = (moving[sign].astype(f32) + low.astype(f32)).astype(bf16)
                else:
                    high = (moving[sign].astype(f32) + high.astype(f32)).astype(bf16)
                out[sign] = jnp.concatenate([low, high], axis=0)
        return out

    def finish(self, parts, moving, halves=False, hook=None, first=2):
        for s in range(first, self.half + 1):
            moving = self.added(parts, moving, s)
            if hook:
                moving = hook(s, moving)
            moving = self.hop(moving)
        if hook:
            moving = hook(self.half + 1, moving)
        total = parts[0].astype(f32)
        for block in moving.values():
            total = total + block.astype(f32)
        return total


def bits_of(size):
    return [1 << b for b in range(size.bit_length() - 1)]


def swap(x, axis, bit):
    return lax.ppermute(x, axis, [(i, i ^ bit) for i in range(lax.axis_size(axis))])


def gather_bits(x, axis, holds=()):
    index = lax.axis_index(axis)
    out = x[None]
    for k, bit in enumerate(reversed(bits_of(lax.axis_size(axis)))):
        came = swap(out, axis, bit)
        if k < len(holds):
            came = after(came, holds[k])
        high = (index & bit) != 0
        out = jnp.stack([jnp.where(high, came, out), jnp.where(high, out, came)], axis=1)
        out = out.reshape((-1,) + x.shape)
    return out


class Fold:
    def __init__(self, x, axis):
        self.x, self.axis = x, axis
        self.left = bits_of(lax.axis_size(axis))

    def send(self):
        pairs = self.x.reshape((-1, 2) + self.x.shape[1:])
        bit = self.left.pop(0)
        high = (lax.axis_index(self.axis) & bit) != 0
        self.keep = jnp.where(high, pairs[:, 1], pairs[:, 0])
        return swap(jnp.where(high, pairs[:, 0], pairs[:, 1]), self.axis, bit)

    def add(self, came):
        self.x = (self.keep.astype(f32) + came.astype(f32)).astype(bf16)

    def finish(self):
        while self.left:
            self.add(self.send())
        return self.x[0]


class Sum:
    def __init__(self, x):
        self.total = x
        self.left = [
            (axis, bit)
            for axis in ("expert", "wshard")
            for bit in reversed(bits_of(lax.axis_size(axis)))
        ]

    def step(self):
        if self.left:
            self.total = self.total + swap(self.total, *self.left.pop(0))
        return self.total

    def finish(self):
        while self.left:
            self.step()
        return self.total


class Group:
    def __init__(self, split):
        self.owners = lax.axis_size("expert")
        self.split = split
        self.far = lax.axis_size("wshard") // 2
        self.rel = [0]
        for bit in reversed(bits_of(self.owners)):
            self.rel += [r ^ bit for r in self.rel]

    def far_block(self, x):
        return [swap(x, "wshard", self.far)] if self.split == 2 else []

    def join(self, own, far):
        if far:
            own = [block for pair in zip(own, far) for block in pair]
        return jnp.concatenate(own, axis=0)

    def gather(self, x, hook=None):
        blocks = [x]
        for bit in reversed(bits_of(self.owners)):
            came = [swap(b, "expert", bit) for b in blocks]
            if hook:
                came = hook(came)
            blocks += came
        return blocks

    def begin(self, send):
        return swap(send, "expert", 1)

    def scatter(self, keep, send=None, came=None):
        bits = bits_of(self.owners)
        came = self.begin(send) if came is None else came
        x = keep.astype(f32) + came.astype(f32)
        for bit in bits[1:]:
            half = x.shape[0] // 2
            size = half // self.split if bit == bits[-1] else half
            parts = []
            for start in reversed(range(0, half, size)):
                part = x[half + start : half + start + size].astype(bf16)
                parts.append(x[start : start + size] + swap(part, "expert", bit).astype(f32))
            x = parts[0] if len(parts) == 1 else parts[::-1]
        return x if isinstance(x, list) else [x]

    def exchange(self, x):
        x = x.reshape((self.owners, self.split, -1) + x.shape[1:])
        came = [
            lax.ppermute(x[k], "expert", [(i, i ^ r) for i in range(self.owners)]) if r else x[k]
            for k, r in enumerate(self.rel)
        ]
        return jnp.stack(came, axis=1)


def expert_kernel(expert, turn, n, owner, m_ref, x_hbm, g_hbm, *refs):
    weights, refs = refs[:n], refs[n:]
    mg_ref, mixing_ref, refs = refs[0], refs[1], refs[2:]
    ends, grads, refs = refs[:2], refs[2 : n + 2], refs[n + 2 :]
    x_ref, g_ref, y_ref, dx_ref, w_ref, d_ref, mixed_ref, gate_ref, up_ref = refs[:9]
    in_sem, w_sem, end_sem, d_sem = refs[9:]
    rows, model = x_ref.shape
    width = w_ref.shape[1]
    count = owner.shape[0] - 1
    depth = model // count
    tile = min(rows, 512)
    routing = m_ref.shape[0] == model
    starts = [sum(w.shape[0] for w in weights[:j]) for j in range(n)] + [w_ref.shape[0]]
    places = []
    for k in range(count):
        at = pl.ds(pl.multiple_of(owner[k] * depth, depth), depth)
        places.append((at, [pl.ds((3 * k + part) * depth, depth) for part in range(3)]))
    source = {start // (3 * depth): j for j, start in enumerate(starts[:-1])}
    final = {start // (3 * depth) - 1: j for j, start in enumerate(starts[1:])}
    copy = pltpu.make_async_copy

    def fetch(k, what):
        at = pl.ds(k * tile, tile)
        from_hbm, to = ((x_hbm, x_ref), (g_hbm, g_ref))[what]
        return copy(from_hbm.at[at], to.at[at], in_sem.at[what, k])

    def fetch_weight(j):
        here = pl.ds(starts[j], weights[j].shape[0])
        return copy(weights[j].at[:, pl.ds(turn * width, width)], w_ref.at[here], w_sem.at[j])

    def finish(k, e):
        at = places[k][0]
        return copy((y_ref, dx_ref)[e].at[:, at], ends[e].at[:, at], end_sem.at[e, k])

    def put(j):
        here = pl.ds(starts[j], weights[j].shape[0])
        return copy(d_ref.at[here], grads[j], d_sem.at[j])

    for what in range(2):
        fetch(0, what).start()
    for j in range(n):
        fetch_weight(j).start()
    for k in range(1, rows // tile):
        for what in range(2):
            fetch(k, what).start()

    for start in range(0, rows, tile):
        here = pl.ds(start, tile)
        for what in range(2):
            fetch(start // tile, what).wait()
        gate = up = back = logits = None
        for k, (at, parts) in enumerate(places):
            if start == 0 and k in source:
                fetch_weight(source[k]).wait()
            x, g = x_ref[here, at], g_ref[here, at]
            a, b, c = mm(x, w_ref[parts[0]]), mm(x, w_ref[parts[1]]), mm(g, w_ref[parts[2]])
            gate, up, back = (a, b, c) if k == 0 else (gate + a, up + b, back + c)
            if routing:
                a = mm(x, m_ref[at])
                logits = a if k == 0 else logits + a
        if routing:
            named = g_ref[here, model:].astype(f32) > 0.0
            top = jnp.max(jnp.where(named, logits, -1e30), axis=1, keepdims=True)
            lifted = jnp.where(named, jnp.exp(jnp.minimum(logits - top, 0.0)), 0.0)
            mixing = lifted * (1.0 / jnp.sum(lifted, axis=1, keepdims=True))
            mixing_ref[here] = mixing
        else:
            mixing = m_ref[here]
        lanes = lax.broadcasted_iota(jnp.int32, mixing.shape, 1)
        mine = jnp.where(lanes == owner[count] + expert, mixing, 0.0)
        mix = jnp.sum(mine, axis=1, keepdims=True)
        sig = 1.0 / (1.0 + jnp.exp(-gate))
        act = gate * sig
        hidden = act * up
        mg_ref[here] = jnp.sum(hidden * back, axis=1, keepdims=True)
        mixed_ref[here] = (mix * hidden).astype(bf16)
        hidden_grad = mix * back
        gate_ref[here] = (hidden_grad * up * sig * (1.0 + gate * (1.0 - sig))).astype(bf16)
        up_ref[here] = (hidden_grad * act).astype(bf16)
    if not routing:
        mixing_ref[...] = jnp.zeros_like(mixing_ref)

    mixed, gate_grad, up_grad = mixed_ref[...], gate_ref[...], up_ref[...]
    for k, (at, parts) in enumerate(places):
        y_ref[:, at] = mm(mixed, w_ref[parts[2]], NT).astype(bf16)
        dx = mm(gate_grad, w_ref[parts[0]], NT) + mm(up_grad, w_ref[parts[1]], NT)
        dx_ref[:, at] = dx.astype(bf16)
        for e in range(2):
            finish(k, e).start()
        x, g = x_ref[:, at], g_ref[:, at]
        d_ref[parts[0]] = mm(x, gate_grad, TN).astype(bf16)
        d_ref[parts[1]] = mm(x, up_grad, TN).astype(bf16)
        d_ref[parts[2]] = mm(g, mixed, TN).astype(bf16)
        if k in final:
            put(final[k]).start()
    for k in range(count):
        for e in range(2):
            finish(k, e).wait()
    for j in range(n):
        put(j).wait()


def expert_pass(expert, turn, turns, owner, x, g, mix, weights):
    n = len(weights)
    rows, model = x.shape
    deep, width = sum(w.shape[0] for w in weights), weights[0].shape[1] // turns
    anywhere, vmem = pl.BlockSpec(memory_space=pl.ANY), pl.BlockSpec(memory_space=pltpu.VMEM)
    count = owner.shape[0] - 1
    out = pl.pallas_call(
        functools.partial(expert_kernel, expert, turn, n),
        in_specs=[pl.BlockSpec(memory_space=pltpu.SMEM), vmem] + [anywhere] * (2 + n),
        out_specs=[vmem, vmem] + [anywhere] * (2 + n),
        scratch_shapes=[
            pltpu.VMEM((rows, model), bf16),
            pltpu.VMEM((rows, g.shape[1]), bf16),
            pltpu.VMEM((rows, model), bf16),
            pltpu.VMEM((rows, model), bf16),
            pltpu.VMEM((deep, width), bf16),
            pltpu.VMEM((deep, width), bf16),
            pltpu.VMEM((rows, width), bf16),
            pltpu.VMEM((rows, width), bf16),
            pltpu.VMEM((rows, width), bf16),
            pltpu.SemaphoreType.DMA((2, -(-rows // 512))),
            pltpu.SemaphoreType.DMA((n,)),
            pltpu.SemaphoreType.DMA((2, count)),
            pltpu.SemaphoreType.DMA((n,)),
        ],
        out_shape=[
            jax.ShapeDtypeStruct((rows, 1), f32),
            jax.ShapeDtypeStruct((rows if mix.shape[0] == model else 8, 128), f32),
        ]
        + [jax.ShapeDtypeStruct((rows, model), bf16)] * 2
        + [jax.ShapeDtypeStruct((w.shape[0], width), bf16) for w in weights],
        compiler_params=pltpu.CompilerParams(vmem_limit_bytes=60 << 20),
        cost_estimate=pl.CostEstimate(
            flops=18 * rows * model * width, transcendentals=0, bytes_accessed=4 * deep * width
        ),
    )(owner, mix, x, g, *weights)
    return list(out[2:4]), out[0], out[1], list(out[4:])


def inverse_rms(values):
    return lax.rsqrt(jnp.mean(values * values, axis=-1, keepdims=True) + epsilon)


def norm_back(values, inverse, gain_vector, grad_rows):
    scaled = values * inverse
    weighted = grad_rows * gain_vector
    return inverse * (weighted - scaled * jnp.mean(weighted * scaled, axis=-1, keepdims=True))


def rotate(values, cosine, sine):
    return values * cosine + pltpu.roll(values, HEAD_DIM // 2, 1) * sine


def each_block(count, size, body):
    def one(k, carry):
        body(pl.ds(pl.multiple_of(k * size, size), size))
        return carry

    lax.fori_loop(0, count // size, one, 0)


def row_places(refs):
    starts = [sum(ref.shape[0] for ref in refs[:b]) for b in range(len(refs))]
    return [pl.ds(start, ref.shape[0]) for start, ref in zip(starts, refs)]


def head_columns(h, part=0, heads=1):
    return pl.ds((part * heads + h) * HEAD_DIM, HEAD_DIM)


def scores_of(low_ref, seg_ref, segs_ref, here, h, heads):
    keys = low_ref[:, head_columns(h, 1, heads)]
    scores = mm(low_ref[here, head_columns(h)], keys, NT) * (1.0 / math.sqrt(HEAD_DIM))
    return jnp.where(seg_ref[here] == segs_ref[...], scores, -1e30)


def attention_kernel(n, heads, block, *refs):
    tokens, refs = refs[:n], refs[n:]
    w_ref, out_ref, gain_ref, qg_ref, kg_ref, cos_ref, sin_ref, seg_ref, segs_ref = refs[:9]
    normed_ref, inverse_ref, raw_ref, low_ref, lse_ref, mixed_ref = refs[9:15]
    parts = refs[15:]
    places = row_places(tokens)
    wide = heads * HEAD_DIM
    for b, here in enumerate(places):
        x = tokens[b][...].astype(f32)
        inverse = inverse_rms(x)
        inverse_ref[here] = inverse
        normed_ref[here] = (x * inverse * gain_ref[...]).astype(bf16)

    def project(here):
        raw = mm(normed_ref[here], w_ref[...])
        raw_ref[here] = raw[:, : 2 * wide]
        low_ref[here, 2 * wide :] = raw[:, 2 * wide :].astype(bf16)
        for part, g_ref in ((0, qg_ref), (1, kg_ref)):
            for h in range(heads):
                at = (part * heads + h) * HEAD_DIM
                u = raw[:, at : at + HEAD_DIM]
                u = u * inverse_rms(u) * g_ref[...]
                low_ref[here, at : at + HEAD_DIM] = rotate(u, cos_ref[here], sin_ref[here]).astype(bf16)

    count = normed_ref.shape[0]
    each_block(count, block, project)

    def attend(here):
        for h in range(heads):
            scores = scores_of(low_ref, seg_ref, segs_ref, here, h, heads)
            top = jnp.max(scores, axis=-1, keepdims=True)
            lifted = jnp.exp(scores - top)
            total = jnp.sum(lifted, axis=-1, keepdims=True)
            probs = (lifted * (1.0 / total)).astype(bf16)
            lse_ref[here, h : h + 1] = top + jnp.log(total)
            mixed_ref[here, head_columns(h)] = mm(
                probs, low_ref[:, head_columns(h, 2, heads)]
            ).astype(bf16)

    each_block(count, block, attend)
    for b, here in enumerate(places):
        parts[b][...] = mm(mixed_ref[here], out_ref[...]).astype(bf16)


def attention_back_kernel(n, heads, block, *refs):
    grads, tokens, refs = refs[:n], refs[n : 2 * n], refs[2 * n :]
    w_ref, out_ref, qg_ref, kg_ref, cos_ref, sin_ref, seg_ref, segs_ref = refs[:8]
    inverse_ref, raw_ref, low_ref, lse_ref = refs[8:12]
    raw_grad_ref, gain_ref, head_gain_ref = refs[12:15]
    parts, refs = refs[15 : 15 + n], refs[15 + n :]
    mixed_ref, query_ref, key_ref, value_ref = refs
    places = row_places(tokens)
    wide = heads * HEAD_DIM
    scale = 1.0 / math.sqrt(HEAD_DIM)
    for b, here in enumerate(places):
        mixed_ref[here] = mm(grads[b][...], out_ref[...], NT).astype(bf16)
    key_ref[...] = jnp.zeros_like(key_ref)
    value_ref[...] = jnp.zeros_like(value_ref)

    def attend(here):
        for h in range(heads):
            at = head_columns(h)
            scores = scores_of(low_ref, seg_ref, segs_ref, here, h, heads)
            probs = jnp.exp(scores - lse_ref[here, h : h + 1])
            mixed_grad = mixed_ref[here, at]
            probs_grad = mm(mixed_grad, low_ref[:, head_columns(h, 2, heads)], NT)
            mean = jnp.sum(probs * probs_grad, axis=-1, keepdims=True)
            scores_grad = (probs * (probs_grad - mean)).astype(bf16)
            query_ref[here, at] = mm(scores_grad, low_ref[:, head_columns(h, 1, heads)]) * scale
            key_ref[:, at] += mm(scores_grad, low_ref[here, at], TN) * scale
            value_ref[:, at] += mm(probs.astype(bf16), mixed_grad, TN)

    count = mixed_ref.shape[0]
    each_block(count, block, attend)
    head_gain_ref[...] = jnp.zeros_like(head_gain_ref)

    def norms_back(here):
        raw_grad_ref[here, 2 * wide :] = value_ref[here].astype(bf16)
        for part, g_ref, rot_ref in ((0, qg_ref, query_ref), (1, kg_ref, key_ref)):
            for h in range(heads):
                at = (part * heads + h) * HEAD_DIM
                grad = rotate(rot_ref[here, head_columns(h)], cos_ref[here], -sin_ref[here])
                u = raw_ref[here, at : at + HEAD_DIM]
                inverse = inverse_rms(u)
                head_gain_ref[part : part + 1] += jnp.sum(
                    grad * (u * inverse), axis=0, keepdims=True
                )
                raw_grad_ref[here, at : at + HEAD_DIM] = norm_back(
                    u, inverse, g_ref[...], grad
                ).astype(bf16)

    each_block(count, block, norms_back)
    gain = None
    for b, here in enumerate(places):
        part = mm(raw_grad_ref[here], w_ref[...], NT)
        parts[b][...] = part.astype(bf16)
        scaled = tokens[b][...].astype(f32) * inverse_ref[here]
        one = jnp.sum(part * scaled, axis=0, keepdims=True)
        gain = one if gain is None else gain + one
    gain_ref[...] = gain


def in_vmem(kernel, shapes, arrays, flops, scratch=()):
    return pl.pallas_call(
        kernel,
        in_specs=[pl.BlockSpec(memory_space=pltpu.VMEM)] * len(arrays),
        out_specs=[pl.BlockSpec(memory_space=pltpu.VMEM)] * len(shapes),
        out_shape=[jax.ShapeDtypeStruct(*shape) for shape in shapes],
        scratch_shapes=list(scratch),
        compiler_params=pltpu.CompilerParams(vmem_limit_bytes=60 << 20),
        cost_estimate=pl.CostEstimate(
            flops=flops,
            transcendentals=0,
            bytes_accessed=sum(a.size * a.dtype.itemsize for a in arrays),
        ),
    )(*arrays)


def local(
    tokens,
    segment_ids,
    routes,
    attn_gain,
    query_weight,
    key_weight,
    value_weight,
    out_weight,
    query_gain,
    key_gain,
    ffn_gain,
    router_weight,
    gate_weight,
    up_weight,
    down_weight,
    d_output,
):
    rows, model = tokens.shape
    owners, shards = lax.axis_size("expert"), lax.axis_size("wshard")
    rank = lax.axis_index("expert")
    local_experts = gate_weight.shape[0]
    experts = local_experts * owners
    heads = HEADS // shards
    wide = heads * HEAD_DIM
    ring = Ring("wshard")
    split = 2 if rows * owners <= 512 else 1
    far = shards // split
    group = Group(split)
    weight_ring = Ring("wshard", split)
    upper = lax.axis_index("wshard") >= far

    held = {}
    quarter = query_weight.shape[0] // owners
    own_rows = jnp.concatenate(
        [
            lax.dynamic_slice_in_dim(w, rank * quarter, quarter)
            .reshape(quarter, shards, wide)
            .transpose(1, 0, 2)
            for w in (query_weight, key_weight, value_weight)
        ],
        axis=2,
    )
    own_columns = lax.all_to_all(own_rows, "wshard", split_axis=0, concat_axis=0, tiled=True)
    named = jnp.sum(
        (routes[:, :, None] == jnp.arange(128, dtype=jnp.int32)).astype(bf16), axis=1
    )
    grad_rows = jnp.concatenate([d_output, named], axis=1)

    def token_hook(s, moving):
        if s == 3:
            moving, held["columns"] = tie(moving, own_columns)
            held["two"] = moving
        if s == ring.half:
            held["last"] = moving
        return moving

    token_blocks = ring.gather(tokens, True, token_hook)
    qkv_weight = gather_bits(held["columns"], "expert", [held["last"]])
    qkv_weight = qkv_weight.transpose(1, 0, 2, 3).reshape(model, 3 * wide)
    grad_own = group.gather(after(grad_rows, held["two"]))

    weights, _ = tie((gate_weight, up_weight, down_weight), held["two"])
    packed = [
        jnp.concatenate([weights[0][i], weights[1][i], weights[2][i].T], axis=0)
        for i in range(local_experts)
    ]
    half = packed[0].shape[1] // 2

    def cross(i, start):
        if split == 1:
            return packed[i][:0]
        send = jnp.where(upper, packed[i][:, :half], packed[i][:, half:])
        return swap(after(send, start), "wshard", far)

    def crossed(i, came):
        if split == 1:
            return packed[i]
        return jnp.concatenate(
            [jnp.where(upper, packed[i][:, half:], packed[i][:, :half]), came], axis=0
        )

    halves = split == 2
    block_owner = weight_ring.owner
    if split == 2:
        block_owner = jnp.stack([block_owner, block_owner ^ far], axis=1).reshape(-1)
    cross_first, cross_second = cross(0, token_blocks[-1]), cross(1, token_blocks[-1])

    sequence = rows * shards
    position = (ring.owner[:, None] * rows + jnp.arange(rows, dtype=jnp.int32)).reshape(-1)
    frequency = rope_base ** (-2.0 * jnp.arange(HEAD_DIM // 2, dtype=f32) / HEAD_DIM)
    angles = position.astype(f32)[:, None] * frequency[None, :]
    cosine, sine = jnp.cos(angles), jnp.sin(angles)
    tables = (
        jnp.concatenate([cosine, cosine], axis=1),
        jnp.concatenate([-sine, sine], axis=1),
    )
    segments = segment_ids.reshape(shards, rows)[ring.owner].reshape(-1)
    segments = (segments[:, None], segments[None, :])
    gains = (query_gain[None], key_gain[None])
    tile = 256
    normed_all, inverse_all, raw, low, log_total, mixed, *attended_part = in_vmem(
        functools.partial(attention_kernel, len(token_blocks), heads, tile),
        [
            ((sequence, model), bf16),
            ((sequence, 1), f32),
            ((sequence, 2 * wide), f32),
            ((sequence, 3 * wide), bf16),
            ((sequence, heads), f32),
            ((sequence, wide), bf16),
        ]
        + [(block.shape, bf16) for block in token_blocks],
        [*token_blocks, qkv_weight, out_weight, attn_gain[None], *gains, *tables, *segments],
        8 * sequence * wide * (4 * model + 2 * sequence),
    )
    attended_part, cross_first, cross_second, grad_own = tie(
        attended_part, cross_first, cross_second, grad_own
    )
    grad_far = group.far_block(after(grad_rows, attended_part[0]))
    first_block = crossed(0, cross_first)
    last_hop = weight_ring.half

    def attended_hook(s, moving):
        if s == 2:
            held["a2"] = moving
            held["send"] = after(first_block, moving)
            if last_hop == 2:
                held["near"] = weight_ring.hop({1: held["send"], -1: held["send"]})
        if s == 3:
            moving, held["grad"] = tie(moving, grad_far)
        if s == ring.half:
            moving, held["near"] = tie(moving, held.get("near"))
        return moving

    attended = ring.finish(
        attended_part, ring.begin(attended_part, True), True, hook=attended_hook
    )
    near = 2 * weight_ring.half - 1
    grad_far = [b for block in held["grad"] for b in group.gather(block)]

    stream = tokens.astype(f32)
    middle = stream + attended
    ffn_inverse = inverse_rms(middle)
    ffn_low = (middle * ffn_inverse * ffn_gain).astype(bf16)

    ffn_far = group.far_block(ffn_low)
    ffn_own = group.gather(ffn_low)
    first_weights = weight_ring.gather(held["send"], halves, first=held["near"])
    ffn_far, first_weights[near:] = tie(ffn_far, first_weights[near:])
    second_block = crossed(1, after(cross_second, ffn_far or ffn_low))

    second_near = weight_ring.hop({1: second_block, -1: second_block})
    ffn_far = [b for block in ffn_far for b in group.gather(block)]
    ffn_all = group.join(ffn_own, ffn_far)
    grad_and_names = group.join(grad_own, grad_far)
    ffn_all, first_weights = tie(ffn_all, first_weights)
    router = jnp.pad(router_weight, ((0, 0), (0, 128 - experts)))
    block_owner = jnp.concatenate([block_owner, rank[None] * local_experts])
    depth = gate_weight.shape[1]

    def uncross(total):
        if split == 1:
            return total[:0]
        return swap(total[3 * depth :].astype(bf16), "wshard", far)

    turns = 2
    call = functools.partial(expert_pass, owner=block_owner, x=ffn_all, g=grad_and_names)

    def part_call(expert, turn, mix, weights):
        return call(expert, turn, turns, mix=mix, weights=weights)

    (end00, mg00, mixing, parts00), second_near = tie(
        part_call(0, 0, router, first_weights), second_near
    )
    second_weights = weight_ring.gather(second_block, halves, first=second_near)
    m00 = weight_ring.begin(parts00, halves)
    (end01, mg01, _, parts01), second_weights, m00 = tie(
        part_call(0, 1, mixing, first_weights), second_weights, m00
    )
    m00 = weight_ring.hop(weight_ring.added(parts00, m00, 2))
    m01 = weight_ring.begin(parts01, halves)
    (end10, mg10, _, parts10), m00, m01 = tie(
        part_call(1, 0, mixing, second_weights), m00, m01
    )
    m01 = weight_ring.hop(weight_ring.added(parts01, m01, 2))
    m10 = weight_ring.begin(parts10, halves)
    sum00 = weight_ring.finish(parts00, m00, halves, first=3)
    home00 = uncross(sum00)
    (end11, mg11, _, parts11), m01, m10, home00 = tie(
        part_call(1, 1, mixing, second_weights), m01, m10, home00
    )

    def ends(which, begin):
        count = ffn_all.shape[0] // 2
        return sum(
            end[which][begin * count : (begin + 1) * count].astype(f32)
            for end in (end00, end01, end10, end11)
        )

    which = jnp.arange(experts, dtype=jnp.int32)[None, :]
    came = group.exchange(jnp.concatenate([mg00 + mg01, mg10 + mg11], axis=1))

    def far_sum(blocks, hold):
        if split == 1:
            return blocks[0]
        send = after(blocks[1].astype(bf16), hold)
        return blocks[0] + swap(send, "wshard", far).astype(f32)

    row_grads = group.scatter(ends(1, 0), ends(1, 1).astype(bf16))
    ffn_grad = far_sum(row_grads, came)
    if split == 2:
        came_far = swap(after(came[1], row_grads[-1]), "wshard", far)
        came = came[0] + after(came_far, row_grads[-1])
    else:
        came = came[0]
    mixing_own = mixing[:rows, :experts]
    mixing_grad = jnp.zeros_like(mixing_own)
    for k, r in enumerate(group.rel):
        block = came[k]
        for i in range(local_experts):
            at = which == (rank ^ r) * local_experts + i
            mixing_grad = jnp.where(at, block[:, i : i + 1], mixing_grad)

    logits_grad = mixing_own * (
        mixing_grad - jnp.sum(mixing_own * mixing_grad, axis=1, keepdims=True)
    )
    router_grad = lax.dot_general(
        logits_grad, ffn_low.astype(f32), TN, precision=highest, preferred_element_type=f32
    )
    ffn_grad = ffn_grad + lax.dot_general(
        logits_grad, router_weight.astype(f32), NT, precision=highest, preferred_element_type=f32
    )
    ffn_gain_grad = jnp.sum(ffn_grad * (middle * ffn_inverse), axis=0)
    middle_grad = d_output.astype(f32) + norm_back(middle, ffn_inverse, ffn_gain, ffn_grad)
    attended_low = middle_grad.astype(bf16)

    def uncrossed(total, other):
        if split == 1:
            return total
        own, other = total[: 3 * depth], other.astype(f32)
        return jnp.concatenate(
            [jnp.where(upper, other, own), jnp.where(upper, own, other)], axis=1
        )

    def middle_hook(s, moving):
        if s == 2:
            held["m11"] = weight_ring.begin(after(parts11, moving), halves)
        if s == 3:
            moving, held["y"] = tie(moving, held["y"])
        if s == ring.half:
            moving, held["m11"] = tie(moving, held["m11"])
        return moving

    end00, end01, end10, end11 = after((end00, end01, end10, end11), attended_low)
    held["y"] = group.scatter(ends(0, 0), ends(0, 1).astype(bf16))

    attended_blocks = ring.gather(attended_low, True, middle_hook)
    attended_blocks, produced = tie(attended_blocks, held["y"])
    expert_out = far_sum(produced, attended_blocks[-1])
    sum01 = weight_ring.finish(parts01, m01, halves, first=3)
    home01 = uncross(after(sum01, attended_blocks[-1]))
    parts10 = after(parts10, attended_blocks[-1])
    second_moving = [
        weight_ring.hop(weight_ring.added(parts10, m10, 2)),
        weight_ring.hop(weight_ring.added(parts11, held["m11"], 2)),
    ]
    raw_grad, attn_gain_grad, head_gain_grad, *normed_part = in_vmem(
        functools.partial(attention_back_kernel, len(token_blocks), heads, tile),
        [((sequence, 3 * wide), bf16), ((1, model), f32), ((2, HEAD_DIM), f32)]
        + [(block.shape, bf16) for block in token_blocks],
        [*attended_blocks, *token_blocks, qkv_weight, out_weight, *gains, *tables, *segments]
        + [inverse_all, raw, low, log_total],
        8 * sequence * wide * (4 * model + 5 * sequence),
        [pltpu.VMEM((sequence, wide), dtype) for dtype in (bf16, f32, f32, f32)],
    )
    due = (normed_part, raw_grad, attn_gain_grad, head_gain_grad)
    due, second_moving, expert_out, home01 = tie(due, second_moving, expert_out, home01)
    normed_part, raw_grad, attn_gain_grad, head_gain_grad = due
    final_stream = middle + expert_out
    output = final_stream.astype(bf16)
    query_gain_grad, key_gain_grad = head_gain_grad[0], head_gain_grad[1]
    router_size = experts * model
    squares = jnp.stack(
        [jnp.sum(v * v) for v in (middle, final_stream, attended, expert_out)]
    )
    small = Sum(
        jnp.concatenate(
            [
                router_grad.reshape(-1),
                ffn_gain_grad,
                attn_gain_grad[0],
                query_gain_grad,
                key_gain_grad,
                jnp.pad(squares, (0, 124)),
            ]
        ).reshape(-1, 128)
    )

    qkv_grad = mm(normed_all, raw_grad, TN).astype(bf16)
    qkv_grad = qkv_grad.reshape(shards, owners, quarter, 3 * wide).transpose(1, 0, 2, 3)
    fold = Fold(qkv_grad, "expert")
    held["fold"] = fold.send()

    def normed_hook(s, moving):
        if s <= ring.half:
            if s != 3:
                small.step()
            moving, small.total = tie(moving, small.step())
        if s in (2, 3) and held["fold"] is not None:
            moving, came = tie(moving, held["fold"])
            fold.add(came)
            held["fold"] = fold.send() if fold.left else None
        if s == 2:
            held["n2"] = moving
        if s == ring.half + 1:
            held["end"] = moving
        return moving

    normed_grad = ring.finish(normed_part, ring.begin(normed_part, True), True, hook=normed_hook)
    tokens_grad = (
        middle_grad + norm_back(stream, inverse_all[:rows], attn_gain, normed_grad)
    ).astype(bf16)
    if held["fold"] is not None:
        fold.add(held["fold"])
    qkv_grad = after(fold.finish(), small.total)
    qkv_grad = lax.all_to_all(qkv_grad, "wshard", split_axis=0, concat_axis=0, tiled=True)
    qkv_grad = gather_bits(qkv_grad, "expert")
    query_weight_grad, key_weight_grad, value_weight_grad = [
        qkv_grad[..., i * wide : (i + 1) * wide]
        .transpose(0, 2, 1, 3)
        .reshape(owners * quarter, model)
        .astype(f32)
        for i in range(3)
    ]
    out_grad = mm(mixed, after(jnp.concatenate(attended_blocks, axis=0), held["n2"]), TN)
    out_grad = Fold(out_grad.astype(bf16).reshape(owners, -1, model), "expert").finish()
    out_grad = gather_bits(out_grad, "expert").reshape(-1, model).astype(f32)

    second_sum = jnp.concatenate(
        [
            weight_ring.finish(parts, moving, halves, first=3)
            for parts, moving in zip((parts10, parts11), second_moving)
        ],
        axis=1,
    )
    second_home = uncross(after(second_sum, held["end"]))
    first_sum = jnp.concatenate([sum00, sum01], axis=1)
    first_home = jnp.concatenate([home00, home01], axis=1)
    summed = [uncrossed(first_sum, first_home), uncrossed(second_sum, second_home)]
    gate_weight_grad = jnp.stack([s[:depth] for s in summed])
    up_weight_grad = jnp.stack([s[depth : 2 * depth] for s in summed])
    down_weight_grad = jnp.stack([s[2 * depth :].T for s in summed])

    small_sums = small.finish().reshape(-1)
    sizes = [router_size, model, model, HEAD_DIM, HEAD_DIM, 4]
    starts = [sum(sizes[:k]) for k in range(len(sizes))]
    router_sum, ffn_gain_grad, attn_gain_grad, query_gain_grad, key_gain_grad, squares = [
        small_sums[a : a + b] for a, b in zip(starts, sizes)
    ]
    router_weight_grad = router_sum.reshape(experts, model).T
    stream_rms = jnp.sqrt(squares / (rows * owners * shards * model))
    return (
        output,
        tokens_grad,
        attn_gain_grad,
        query_weight_grad,
        key_weight_grad,
        value_weight_grad,
        out_grad,
        query_gain_grad,
        key_gain_grad,
        ffn_gain_grad,
        router_weight_grad,
        gate_weight_grad,
        up_weight_grad,
        down_weight_grad,
        stream_rms,
    )


def solution(mesh):
    rows = P(("expert", "wshard"), None)
    shard = P("wshard", None)
    wide = P("expert", "wshard", None)
    tall = P("expert", None, "wshard")
    return jax.shard_map(
        local,
        mesh=mesh,
        in_specs=(rows, P("expert"), rows, P(), shard, shard, shard, shard)
        + (P(), P(), P(), P(), wide, wide, tall, rows),
        out_specs=(rows, rows, P(), shard, shard, shard, shard)
        + (P(), P(), P(), P(), wide, wide, tall, P()),
        check_vma=False,
    )
```

```python
import functools
import math

import jax
import jax.numpy as jnp
from jax import lax
from jax.experimental import pallas as pl
from jax.experimental.pallas import tpu as pltpu
from jax.sharding import PartitionSpec as P

HEADS = 16
HEAD_DIM = 128
epsilon = 1e-06
rope_base = 50000.0
highest = lax.Precision.HIGHEST
bf16 = jnp.bfloat16
f32 = jnp.float32

NN = (((1,), (0,)), ((), ()))
NT = (((1,), (1,)), ((), ()))
TN = (((0,), (0,)), ((), ()))


def mm(a, b, dims=NN):
    return lax.dot_general(a, b, dims, preferred_element_type=f32)


def tie(*arrays):
    return lax.optimization_barrier(arrays)


def after(x, *others):
    return lax.optimization_barrier((x, others))[0]


def ring_order(n):
    return list(range(0, n, 2)) + list(range(n - 1, 0, -2))


class Ring:
    def __init__(self, axis, groups=1):
        self.axis = axis
        total = lax.axis_size(axis)
        n = total // groups
        order = ring_order(n)
        self.down = [
            (g * n + order[i], g * n + order[(i + 1) % n]) for g in range(groups) for i in range(n)
        ]
        self.up = [(b, a) for a, b in self.down]
        place = [order.index(w % n) for w in range(total)]
        here = jnp.asarray(place, jnp.int32)[lax.axis_index(axis)]
        self.half = n // 2
        self.offsets = [0]
        for s in range(1, self.half):
            self.offsets += [-s, s]
        self.offsets.append(-self.half)
        table = jnp.asarray(order, jnp.int32)
        first = lax.axis_index(axis) // n * n
        self.owner = first + table[(here + jnp.asarray(self.offsets, jnp.int32) + n) % n]

    def hop(self, moving):
        return {
            sign: lax.ppermute(block, self.axis, self.down if sign == 1 else self.up)
            for sign, block in moving.items()
        }

    def gather(self, own, halves=False, hook=None, first=None):
        got = {0: own}
        moving = {1: own, -1: own}
        for s in range(1, self.half + 1):
            if s == self.half:
                if halves:
                    middle = own.shape[0] // 2
                    moving = {1: moving[1][:middle], -1: moving[-1][middle:]}
                else:
                    moving.pop(-1)
            if hook:
                moving = hook(s, moving)
            moving = first if s == 1 and first else self.hop(moving)
            for sign, block in moving.items():
                got[-s * sign] = block
        blocks = [got[o] for o in self.offsets]
        return blocks + [moving[-1]] if halves else blocks

    def begin(self, parts, halves=False):
        moving = {1: parts[2 * self.half - 1]}
        if halves:
            moving[-1] = parts[-1]
        return self.hop(moving)

    def scatter(self, parts, halves=False, hook=None):
        return self.finish(parts, self.begin(parts, halves), halves, hook)

    def added(self, parts, moving, s):
        part = dict(zip(self.offsets, parts))
        distance = self.half - s + 1
        out = {}
        for sign in (1, -1):
            own = part[sign * distance]
            if sign not in moving:
                out[sign] = own
            elif moving[sign].shape == own.shape:
                out[sign] = (moving[sign].astype(f32) + own.astype(f32)).astype(bf16)
            else:
                middle = own.shape[0] // 2
                low, high = own[:middle], own[middle:]
                if sign == 1:
                    low = (moving[sign].astype(f32) + low.astype(f32)).astype(bf16)
                else:
                    high = (moving[sign].astype(f32) + high.astype(f32)).astype(bf16)
                out[sign] = jnp.concatenate([low, high], axis=0)
        return out

    def finish(self, parts, moving, halves=False, hook=None, first=2):
        for s in range(first, self.half + 1):
            moving = self.added(parts, moving, s)
            if hook:
                moving = hook(s, moving)
            moving = self.hop(moving)
        if hook:
            moving = hook(self.half + 1, moving)
        total = parts[0].astype(f32)
        for block in moving.values():
            total = total + block.astype(f32)
        return total


def bits_of(size):
    return [1 << b for b in range(size.bit_length() - 1)]


def swap(x, axis, bit):
    return lax.ppermute(x, axis, [(i, i ^ bit) for i in range(lax.axis_size(axis))])


def gather_bits(x, axis, holds=()):
    index = lax.axis_index(axis)
    out = x[None]
    for k, bit in enumerate(reversed(bits_of(lax.axis_size(axis)))):
        came = swap(out, axis, bit)
        if k < len(holds):
            came = after(came, holds[k])
        high = (index & bit) != 0
        out = jnp.stack([jnp.where(high, came, out), jnp.where(high, out, came)], axis=1)
        out = out.reshape((-1,) + x.shape)
    return out


class Fold:
    def __init__(self, x, axis):
        self.x, self.axis = x, axis
        self.left = bits_of(lax.axis_size(axis))

    def send(self):
        pairs = self.x.reshape((-1, 2) + self.x.shape[1:])
        bit = self.left.pop(0)
        high = (lax.axis_index(self.axis) & bit) != 0
        self.keep = jnp.where(high, pairs[:, 1], pairs[:, 0])
        return swap(jnp.where(high, pairs[:, 0], pairs[:, 1]), self.axis, bit)

    def add(self, came):
        self.x = (self.keep.astype(f32) + came.astype(f32)).astype(bf16)

    def finish(self):
        while self.left:
            self.add(self.send())
        return self.x[0]


class Sum:
    def __init__(self, x):
        self.total = x
        self.left = [
            (axis, bit)
            for axis in ("expert", "wshard")
            for bit in reversed(bits_of(lax.axis_size(axis)))
        ]

    def step(self):
        if self.left:
            self.total = self.total + swap(self.total, *self.left.pop(0))
        return self.total

    def finish(self):
        while self.left:
            self.step()
        return self.total


class Group:
    def __init__(self, split):
        self.owners = lax.axis_size("expert")
        self.split = split
        self.far = lax.axis_size("wshard") // 2
        self.rel = [0]
        for bit in reversed(bits_of(self.owners)):
            self.rel += [r ^ bit for r in self.rel]

    def far_block(self, x):
        return [swap(x, "wshard", self.far)] if self.split == 2 else []

    def join(self, own, far):
        if far:
            own = [block for pair in zip(own, far) for block in pair]
        return jnp.concatenate(own, axis=0)

    def gather(self, x, hook=None):
        blocks = [x]
        for bit in reversed(bits_of(self.owners)):
            came = [swap(b, "expert", bit) for b in blocks]
            if hook:
                came = hook(came)
            blocks += came
        return blocks

    def begin(self, send):
        return swap(send, "expert", 1)

    def scatter(self, keep, send=None, came=None):
        bits = bits_of(self.owners)
        came = self.begin(send) if came is None else came
        x = keep.astype(f32) + came.astype(f32)
        for bit in bits[1:]:
            half = x.shape[0] // 2
            size = half // self.split if bit == bits[-1] else half
            parts = []
            for start in reversed(range(0, half, size)):
                part = x[half + start : half + start + size].astype(bf16)
                parts.append(x[start : start + size] + swap(part, "expert", bit).astype(f32))
            x = parts[0] if len(parts) == 1 else parts[::-1]
        return x if isinstance(x, list) else [x]


def expert_kernel(expert, turn, first, last, n, owner, m_ref, x_hbm, g_hbm, *refs):
    weights, refs = refs[:n], refs[n:]
    before, refs = ((), refs) if first else (refs[:2], refs[2:])
    state_ref, refs = refs[0], refs[1:]
    k = 2 if last else 1
    ends, refs = (refs[:k], refs[k : 2 * k]), refs[2 * k :]
    grads, refs = refs[:n], refs[n:]
    x_ref, g_ref, y_ref, dx_ref, w_ref, d_ref, mixed_ref, gate_ref, up_ref = refs[:9]
    old_refs = refs[9:11]
    in_sem, w_sem, end_sem, d_sem, old_sem = refs[11:]
    rows, model = x_ref.shape
    width = w_ref.shape[1]
    count = owner.shape[0] - 1
    depth = model // count
    tile = min(rows, 512)
    starts = [sum(w.shape[0] for w in weights[:j]) for j in range(n)] + [w_ref.shape[0]]
    places = []
    for k in range(count):
        at = pl.ds(pl.multiple_of(owner[k] * depth, depth), depth)
        places.append((at, [pl.ds((3 * k + part) * depth, depth) for part in range(3)]))
    source = {start // (3 * depth): j for j, start in enumerate(starts[:-1])}
    final = {start // (3 * depth) - 1: j for j, start in enumerate(starts[1:])}
    copy = pltpu.make_async_copy

    def fetch(k, what):
        at = pl.ds(k * tile, tile)
        from_hbm, to = ((x_hbm, x_ref), (g_hbm, g_ref))[what]
        return copy(from_hbm.at[at], to.at[at], in_sem.at[what, k])

    def fetch_weight(j):
        here = pl.ds(starts[j], weights[j].shape[0])
        return copy(weights[j].at[:, pl.ds(turn * width, width)], w_ref.at[here], w_sem.at[j])

    def finish(k):
        at = places[k][0] if k < count else pl.ds(model, 128)
        copies = []
        for what, (ref, parts) in enumerate(zip((y_ref, dx_ref), ends)):
            half = rows // len(parts)
            for e, to in enumerate(parts):
                if k < count or what == 1:
                    rows_at = pl.ds(e * half, half)
                    sem = end_sem.at[2 * what + e, k]
                    copies.append(copy(ref.at[rows_at, at], to.at[:, at], sem))
        return copies

    def put(j):
        here = pl.ds(starts[j], weights[j].shape[0])
        return copy(d_ref.at[here], grads[j], d_sem.at[j])

    for what in range(2):
        fetch(0, what).start()
    for j in range(n):
        fetch_weight(j).start()
    for k in range(1, rows // tile):
        for what in range(2):
            fetch(k, what).start()

    for what, old in enumerate(before):
        copy(old, old_refs[what], old_sem.at[what]).start()

    for start in range(0, rows, tile):
        here = pl.ds(start, tile)
        for what in range(2):
            fetch(start // tile, what).wait()
        gate = up = back = logits = None
        for k, (at, parts) in enumerate(places):
            if start == 0 and k in source:
                fetch_weight(source[k]).wait()
            x, g = x_ref[here, at], g_ref[here, at]
            a, b, c = mm(x, w_ref[parts[0]]), mm(x, w_ref[parts[1]]), mm(g, w_ref[parts[2]])
            gate, up, back = (a, b, c) if k == 0 else (gate + a, up + b, back + c)
            if first:
                a = mm(x, m_ref[at])
                logits = a if k == 0 else logits + a
        if first:
            named = g_ref[here, model:].astype(f32) > 0.0
            top = jnp.max(jnp.where(named, logits, -1e30), axis=1, keepdims=True)
            lifted = jnp.where(named, jnp.exp(jnp.minimum(logits - top, 0.0)), 0.0)
            state = lifted * (1.0 / jnp.sum(lifted, axis=1, keepdims=True))
        else:
            state = m_ref[here]
        lanes = lax.broadcasted_iota(jnp.int32, state.shape, 1)
        lane = owner[count] + expert
        mix = jnp.sum(jnp.where(lanes == lane, state, 0.0), axis=1, keepdims=True)
        sig = 1.0 / (1.0 + jnp.exp(-gate))
        act = gate * sig
        hidden = act * up
        mixing_grad = jnp.sum(hidden * back, axis=1, keepdims=True)
        state = state + jnp.where(lanes == 64 + lane, mixing_grad, 0.0)
        state_ref[here] = state
        if last:
            state = jnp.where(lanes >= 64, state, 0.0)
            near = state.astype(bf16).astype(f32)
            dx_ref[here, model:] = (near + pltpu.roll(state - near, 32, 1)).astype(bf16)
        mixed_ref[here] = (mix * hidden).astype(bf16)
        hidden_grad = mix * back
        gate_ref[here] = (hidden_grad * up * sig * (1.0 + gate * (1.0 - sig))).astype(bf16)
        up_ref[here] = (hidden_grad * act).astype(bf16)
    for what, old in enumerate(before):
        copy(old, old_refs[what], old_sem.at[what]).wait()
    mixed, gate_grad, up_grad = mixed_ref[...], gate_ref[...], up_ref[...]
    for k, (at, parts) in enumerate(places):
        y = mm(mixed, w_ref[parts[2]], NT)
        dx = mm(gate_grad, w_ref[parts[0]], NT) + mm(up_grad, w_ref[parts[1]], NT)
        if before:
            y = y + old_refs[0][:, at].astype(f32)
            dx = dx + old_refs[1][:, at].astype(f32)
        y_ref[:, at], dx_ref[:, at] = y.astype(bf16), dx.astype(bf16)
        for end in finish(k):
            end.start()
        x, g = x_ref[:, at], g_ref[:, at]
        d_ref[parts[0]] = mm(x, gate_grad, TN).astype(bf16)
        d_ref[parts[1]] = mm(x, up_grad, TN).astype(bf16)
        d_ref[parts[2]] = mm(g, mixed, TN).astype(bf16)
        if k in final:
            put(final[k]).start()
    if last:
        for end in finish(count):
            end.start()
    for k in range(count + last):
        for end in finish(k):
            end.wait()
    for j in range(n):
        put(j).wait()


def expert_pass(expert, turn, first, last, turns, owner, x, g, mix, weights, before):
    n = len(weights)
    rows, model = x.shape
    deep, width = sum(w.shape[0] for w in weights), weights[0].shape[1] // turns
    anywhere, vmem = pl.BlockSpec(memory_space=pl.ANY), pl.BlockSpec(memory_space=pltpu.VMEM)
    count = owner.shape[0] - 1
    k = 2 if last else 1
    wide = model + 128 if last else model
    ends = [jax.ShapeDtypeStruct((rows // k, model), bf16)] * k
    ends += [jax.ShapeDtypeStruct((rows // k, wide), bf16)] * k
    old = pltpu.VMEM((8, 128) if first else (rows, model), bf16)
    out = pl.pallas_call(
        functools.partial(expert_kernel, expert, turn, first, last, n),
        in_specs=[pl.BlockSpec(memory_space=pltpu.SMEM), vmem]
        + [anywhere] * (2 + n + len(before)),
        out_specs=[vmem] + [anywhere] * (2 * k + n),
        scratch_shapes=[
            pltpu.VMEM((rows, model), bf16),
            pltpu.VMEM((rows, g.shape[1]), bf16),
            pltpu.VMEM((rows, model), bf16),
            pltpu.VMEM((rows, wide), bf16),
            pltpu.VMEM((deep, width), bf16),
            pltpu.VMEM((deep, width), bf16),
            pltpu.VMEM((rows, width), bf16),
            pltpu.VMEM((rows, width), bf16),
            pltpu.VMEM((rows, width), bf16),
            old,
            old,
            pltpu.SemaphoreType.DMA((2, -(-rows // 512))),
            pltpu.SemaphoreType.DMA((n,)),
            pltpu.SemaphoreType.DMA((4, count + 1)),
            pltpu.SemaphoreType.DMA((n,)),
            pltpu.SemaphoreType.DMA((2,)),
        ],
        out_shape=[jax.ShapeDtypeStruct((rows, 128), f32)]
        + ends
        + [jax.ShapeDtypeStruct((w.shape[0], width), bf16) for w in weights],
        compiler_params=pltpu.CompilerParams(vmem_limit_bytes=60 << 20),
        cost_estimate=pl.CostEstimate(
            flops=18 * rows * model * width, transcendentals=0, bytes_accessed=4 * deep * width
        ),
    )(owner, mix, x, g, *weights, *before)
    return out[0], list(out[1 : 1 + 2 * k]), list(out[1 + 2 * k :])


def spread_kernel(x_ref, *out_refs):
    owners, shards, rows, columns = x_ref.shape
    wide = columns // len(out_refs)
    for e in range(owners):
        for w in range(shards):
            for i, out_ref in enumerate(out_refs):
                part = x_ref[e, w, :, i * wide : (i + 1) * wide].astype(f32)
                out_ref[e * rows : (e + 1) * rows, w * wide : (w + 1) * wide] = part


def merge_kernel(upper_ref, *refs):
    gate_ref, up_ref, down_ref = refs[-3:]
    half = refs[0].shape[1]
    depth = gate_ref.shape[1]
    upper = upper_ref[0] > 0
    for i in range(gate_ref.shape[0]):
        for part, out_ref in enumerate((gate_ref, up_ref, down_ref)):
            rows = pl.ds(part * depth, depth)
            own, other = refs[2 * i][rows], refs[2 * i + 1][rows].astype(f32)
            low, high = jnp.where(upper, other, own), jnp.where(upper, own, other)
            if part < 2:
                out_ref[i, :, :half], out_ref[i, :, half:] = low, high
            else:
                out_ref[i, :half], out_ref[i, half:] = low.T, high.T


def inverse_rms(values):
    return lax.rsqrt(jnp.mean(values * values, axis=-1, keepdims=True) + epsilon)


def norm_back(values, inverse, gain_vector, grad_rows):
    scaled = values * inverse
    weighted = grad_rows * gain_vector
    return inverse * (weighted - scaled * jnp.mean(weighted * scaled, axis=-1, keepdims=True))


def rotate(values, cosine, sine):
    return values * cosine + pltpu.roll(values, HEAD_DIM // 2, 1) * sine


def each_block(count, size, body):
    def one(k, carry):
        body(pl.ds(pl.multiple_of(k * size, size), size))
        return carry

    lax.fori_loop(0, count // size, one, 0)


def row_places(refs):
    starts = [sum(ref.shape[0] for ref in refs[:b]) for b in range(len(refs))]
    return [pl.ds(start, ref.shape[0]) for start, ref in zip(starts, refs)]


def head_columns(h, part=0, heads=1):
    return pl.ds((part * heads + h) * HEAD_DIM, HEAD_DIM)


def scores_of(low_ref, seg_ref, segs_ref, here, h, heads):
    keys = low_ref[:, head_columns(h, 1, heads)]
    scores = mm(low_ref[here, head_columns(h)], keys, NT) * (1.0 / math.sqrt(HEAD_DIM))
    return jnp.where(seg_ref[here] == segs_ref[...], scores, -1e30)


def attention_kernel(n, heads, block, *refs):
    tokens, refs = refs[:n], refs[n:]
    w_ref, out_ref, gain_ref, qg_ref, kg_ref, cos_ref, sin_ref, seg_ref, segs_ref = refs[:9]
    normed_ref, inverse_ref, raw_ref, low_ref, lse_ref, mixed_ref = refs[9:15]
    parts = refs[15:]
    places = row_places(tokens)
    wide = heads * HEAD_DIM
    for b, here in enumerate(places):
        x = tokens[b][...].astype(f32)
        inverse = inverse_rms(x)
        inverse_ref[here] = inverse
        normed_ref[here] = (x * inverse * gain_ref[...]).astype(bf16)

    def project(here):
        raw = mm(normed_ref[here], w_ref[...])
        raw_ref[here] = raw[:, : 2 * wide]
        low_ref[here, 2 * wide :] = raw[:, 2 * wide :].astype(bf16)
        for part, g_ref in ((0, qg_ref), (1, kg_ref)):
            for h in range(heads):
                at = (part * heads + h) * HEAD_DIM
                u = raw[:, at : at + HEAD_DIM]
                u = u * inverse_rms(u) * g_ref[...]
                low_ref[here, at : at + HEAD_DIM] = rotate(u, cos_ref[here], sin_ref[here]).astype(bf16)

    count = normed_ref.shape[0]
    each_block(count, block, project)

    def attend(here):
        for h in range(heads):
            scores = scores_of(low_ref, seg_ref, segs_ref, here, h, heads)
            top = jnp.max(scores, axis=-1, keepdims=True)
            lifted = jnp.exp(scores - top)
            total = jnp.sum(lifted, axis=-1, keepdims=True)
            probs = (lifted * (1.0 / total)).astype(bf16)
            lse_ref[here, h : h + 1] = top + jnp.log(total)
            mixed_ref[here, head_columns(h)] = mm(
                probs, low_ref[:, head_columns(h, 2, heads)]
            ).astype(bf16)

    each_block(count, block, attend)
    for b, here in enumerate(places):
        parts[b][...] = mm(mixed_ref[here], out_ref[...]).astype(bf16)


def attention_back_kernel(n, heads, block, *refs):
    grads, tokens, refs = refs[:n], refs[n : 2 * n], refs[2 * n :]
    w_ref, out_ref, qg_ref, kg_ref, cos_ref, sin_ref, seg_ref, segs_ref = refs[:8]
    inverse_ref, raw_ref, low_ref, lse_ref = refs[8:12]
    raw_grad_ref, gain_ref, head_gain_ref = refs[12:15]
    parts, refs = refs[15 : 15 + n], refs[15 + n :]
    mixed_ref, query_ref, key_ref, value_ref = refs
    places = row_places(tokens)
    wide = heads * HEAD_DIM
    scale = 1.0 / math.sqrt(HEAD_DIM)
    for b, here in enumerate(places):
        mixed_ref[here] = mm(grads[b][...], out_ref[...], NT).astype(bf16)
    key_ref[...] = jnp.zeros_like(key_ref)
    value_ref[...] = jnp.zeros_like(value_ref)

    def attend(here):
        for h in range(heads):
            at = head_columns(h)
            scores = scores_of(low_ref, seg_ref, segs_ref, here, h, heads)
            probs = jnp.exp(scores - lse_ref[here, h : h + 1])
            mixed_grad = mixed_ref[here, at]
            probs_grad = mm(mixed_grad, low_ref[:, head_columns(h, 2, heads)], NT)
            mean = jnp.sum(probs * probs_grad, axis=-1, keepdims=True)
            scores_grad = (probs * (probs_grad - mean)).astype(bf16)
            query_ref[here, at] = mm(scores_grad, low_ref[:, head_columns(h, 1, heads)]) * scale
            key_ref[:, at] += mm(scores_grad, low_ref[here, at], TN) * scale
            value_ref[:, at] += mm(probs.astype(bf16), mixed_grad, TN)

    count = mixed_ref.shape[0]
    each_block(count, block, attend)
    head_gain_ref[...] = jnp.zeros_like(head_gain_ref)

    def norms_back(here):
        raw_grad_ref[here, 2 * wide :] = value_ref[here].astype(bf16)
        for part, g_ref, rot_ref in ((0, qg_ref, query_ref), (1, kg_ref, key_ref)):
            for h in range(heads):
                at = (part * heads + h) * HEAD_DIM
                grad = rotate(rot_ref[here, head_columns(h)], cos_ref[here], -sin_ref[here])
                u = raw_ref[here, at : at + HEAD_DIM]
                inverse = inverse_rms(u)
                head_gain_ref[part : part + 1] += jnp.sum(
                    grad * (u * inverse), axis=0, keepdims=True
                )
                raw_grad_ref[here, at : at + HEAD_DIM] = norm_back(
                    u, inverse, g_ref[...], grad
                ).astype(bf16)

    each_block(count, block, norms_back)
    gain = None
    for b, here in enumerate(places):
        part = mm(raw_grad_ref[here], w_ref[...], NT)
        parts[b][...] = part.astype(bf16)
        scaled = tokens[b][...].astype(f32) * inverse_ref[here]
        one = jnp.sum(part * scaled, axis=0, keepdims=True)
        gain = one if gain is None else gain + one
    gain_ref[...] = gain


def in_vmem(kernel, shapes, arrays, flops, scratch=(), scalars=0):
    return pl.pallas_call(
        kernel,
        in_specs=[pl.BlockSpec(memory_space=pltpu.SMEM)] * scalars
        + [pl.BlockSpec(memory_space=pltpu.VMEM)] * (len(arrays) - scalars),
        out_specs=[pl.BlockSpec(memory_space=pltpu.VMEM)] * len(shapes),
        out_shape=[jax.ShapeDtypeStruct(*shape) for shape in shapes],
        scratch_shapes=list(scratch),
        compiler_params=pltpu.CompilerParams(vmem_limit_bytes=60 << 20),
        cost_estimate=pl.CostEstimate(
            flops=flops,
            transcendentals=0,
            bytes_accessed=sum(a.size * a.dtype.itemsize for a in arrays),
        ),
    )(*arrays)


def local(
    tokens,
    segment_ids,
    routes,
    attn_gain,
    query_weight,
    key_weight,
    value_weight,
    out_weight,
    query_gain,
    key_gain,
    ffn_gain,
    router_weight,
    gate_weight,
    up_weight,
    down_weight,
    d_output,
):
    rows, model = tokens.shape
    owners, shards = lax.axis_size("expert"), lax.axis_size("wshard")
    rank = lax.axis_index("expert")
    local_experts = gate_weight.shape[0]
    experts = local_experts * owners
    heads = HEADS // shards
    wide = heads * HEAD_DIM
    ring = Ring("wshard")
    split = 2 if rows * owners <= 512 else 1
    far = shards // split
    group = Group(split)
    weight_ring = Ring("wshard", split)
    upper = lax.axis_index("wshard") >= far

    held = {}
    quarter = query_weight.shape[0] // owners
    own_rows = jnp.concatenate(
        [
            lax.dynamic_slice_in_dim(w, rank * quarter, quarter)
            .reshape(quarter, shards, wide)
            .transpose(1, 0, 2)
            for w in (query_weight, key_weight, value_weight)
        ],
        axis=2,
    )
    own_columns = lax.all_to_all(own_rows, "wshard", split_axis=0, concat_axis=0, tiled=True)
    named = jnp.sum(
        (routes[:, :, None] == jnp.arange(128, dtype=jnp.int32)).astype(bf16), axis=1
    )
    grad_rows = jnp.concatenate([d_output, named], axis=1)

    def token_hook(s, moving):
        if s == 3:
            moving, held["columns"] = tie(moving, own_columns)
            held["two"] = moving
        if s == ring.half:
            held["last"] = moving
        return moving

    token_blocks = ring.gather(tokens, True, token_hook)
    qkv_weight = gather_bits(held["columns"], "expert", [held["last"]])
    qkv_weight = qkv_weight.transpose(1, 0, 2, 3).reshape(model, 3 * wide)
    grad_own = group.gather(after(grad_rows, held["two"]))

    weights, _ = tie((gate_weight, up_weight, down_weight), held["two"])
    packed = [
        jnp.concatenate([weights[0][i], weights[1][i], weights[2][i].T], axis=0)
        for i in range(local_experts)
    ]
    half = packed[0].shape[1] // 2

    def cross(i, start):
        if split == 1:
            return packed[i][:0]
        send = jnp.where(upper, packed[i][:, :half], packed[i][:, half:])
        return swap(after(send, start), "wshard", far)

    def crossed(i, came):
        if split == 1:
            return packed[i]
        return jnp.concatenate(
            [jnp.where(upper, packed[i][:, half:], packed[i][:, :half]), came], axis=0
        )

    halves = split == 2
    block_owner = weight_ring.owner
    if split == 2:
        block_owner = jnp.stack([block_owner, block_owner ^ far], axis=1).reshape(-1)
    cross_first, cross_second = cross(0, token_blocks[-1]), cross(1, token_blocks[-1])

    sequence = rows * shards
    position = (ring.owner[:, None] * rows + jnp.arange(rows, dtype=jnp.int32)).reshape(-1)
    frequency = rope_base ** (-2.0 * jnp.arange(HEAD_DIM // 2, dtype=f32) / HEAD_DIM)
    angles = position.astype(f32)[:, None] * frequency[None, :]
    cosine, sine = jnp.cos(angles), jnp.sin(angles)
    tables = (
        jnp.concatenate([cosine, cosine], axis=1),
        jnp.concatenate([-sine, sine], axis=1),
    )
    segments = segment_ids.reshape(shards, rows)[ring.owner].reshape(-1)
    segments = (segments[:, None], segments[None, :])
    gains = (query_gain[None], key_gain[None])
    tile = 256
    normed_all, inverse_all, raw, low, log_total, mixed, *attended_part = in_vmem(
        functools.partial(attention_kernel, len(token_blocks), heads, tile),
        [
            ((sequence, model), bf16),
            ((sequence, 1), f32),
            ((sequence, 2 * wide), f32),
            ((sequence, 3 * wide), bf16),
            ((sequence, heads), f32),
            ((sequence, wide), bf16),
        ]
        + [(block.shape, bf16) for block in token_blocks],
        [*token_blocks, qkv_weight, out_weight, attn_gain[None], *gains, *tables, *segments],
        8 * sequence * wide * (4 * model + 2 * sequence),
    )
    attended_part, cross_first, cross_second, grad_own = tie(
        attended_part, cross_first, cross_second, grad_own
    )
    grad_far = group.far_block(after(grad_rows, attended_part[0]))
    first_block = crossed(0, cross_first)
    last_hop = weight_ring.half

    def attended_hook(s, moving):
        if s == 2:
            held["a2"] = moving
            held["send"] = after(first_block, moving)
            if last_hop == 2:
                held["near"] = weight_ring.hop({1: held["send"], -1: held["send"]})
        if s == 3:
            moving, held["grad"] = tie(moving, grad_far)
        if s == ring.half:
            moving, held["near"] = tie(moving, held.get("near"))
        return moving

    attended = ring.finish(
        attended_part, ring.begin(attended_part, True), True, hook=attended_hook
    )
    near = 2 * weight_ring.half - 1
    grad_far = [b for block in held["grad"] for b in group.gather(block)]

    stream = tokens.astype(f32)
    middle = stream + attended
    ffn_inverse = inverse_rms(middle)
    ffn_low = (middle * ffn_inverse * ffn_gain).astype(bf16)

    ffn_far = group.far_block(ffn_low)
    ffn_own = group.gather(ffn_low)
    first_weights = weight_ring.gather(held["send"], halves, first=held["near"])
    ffn_far, first_weights[near:] = tie(ffn_far, first_weights[near:])
    second_block = crossed(1, after(cross_second, ffn_far or ffn_low))
    second_near = weight_ring.hop({1: second_block, -1: second_block})
    ffn_far = [b for block in ffn_far for b in group.gather(block)]
    ffn_all = group.join(ffn_own, ffn_far)
    grad_and_names = group.join(grad_own, grad_far)
    ffn_all, first_weights = tie(ffn_all, first_weights)
    router = jnp.pad(router_weight, ((0, 0), (0, 128 - experts)))
    block_owner = jnp.concatenate([block_owner, rank[None] * local_experts])
    depth = gate_weight.shape[1]

    def uncross(total):
        if split == 1:
            return total[:0]
        return swap(total[3 * depth :].astype(bf16), "wshard", far)

    turns = 2
    call = functools.partial(expert_pass, owner=block_owner, x=ffn_all, g=grad_and_names)

    def part_call(expert, turn, mix, weights, *before):
        first, last = (expert, turn) == (0, 0), (expert, turn) == (local_experts - 1, turns - 1)
        return call(expert, turn, first, last, turns, mix=mix, weights=weights, before=before)

    (state, ends, parts00), second_near = tie(
        part_call(0, 0, router, first_weights), second_near
    )
    second_weights = weight_ring.gather(second_block, halves, first=second_near)
    m00 = weight_ring.begin(parts00, halves)
    (state, ends, parts01), second_weights, m00 = tie(
        part_call(0, 1, state, first_weights, *ends), second_weights, m00
    )
    m00 = weight_ring.hop(weight_ring.added(parts00, m00, 2))
    m01 = weight_ring.begin(parts01, halves)
    (state, ends, parts10), m00, m01 = tie(
        part_call(1, 0, state, second_weights, *ends), m00, m01
    )
    m01 = weight_ring.hop(weight_ring.added(parts01, m01, 2))
    m10 = weight_ring.begin(parts10, halves)
    (state, ends, parts11), m01, m10 = tie(
        part_call(1, 1, state, second_weights, *ends), m01, m10
    )
    sum00 = weight_ring.finish(parts00, m00, halves, first=3)
    m10 = weight_ring.hop(weight_ring.added(parts10, m10, 2))
    came = group.begin(ends[3])
    y_came = group.begin(after(ends[1], came))
    row_grads = group.scatter(ends[2], came=came)
    row_grads[-1], m10 = tie(row_grads[-1], m10)
    produced = group.scatter(after(ends[0], row_grads[-1]), came=y_came)

    def far_sum(blocks, hold):
        if split == 1:
            return blocks[0]
        send = after(blocks[1].astype(bf16), hold)
        return blocks[0] + swap(send, "wshard", far).astype(f32)

    ffn_grad = far_sum(row_grads, came)
    mixing_grad = ffn_grad[:, model + 64 : model + 64 + experts]
    mixing_grad = mixing_grad + ffn_grad[:, model + 96 : model + 96 + experts]
    ffn_grad = ffn_grad[:, :model]
    mixing_own = state[:rows, :experts]
    logits_grad = mixing_own * (
        mixing_grad - jnp.sum(mixing_own * mixing_grad, axis=1, keepdims=True)
    )
    router_grad = lax.dot_general(
        logits_grad, ffn_low.astype(f32), TN, precision=highest, preferred_element_type=f32
    )
    ffn_grad = ffn_grad + lax.dot_general(
        logits_grad, router_weight.astype(f32), NT, precision=highest, preferred_element_type=f32
    )
    ffn_gain_grad = jnp.sum(ffn_grad * (middle * ffn_inverse), axis=0)
    middle_grad = d_output.astype(f32) + norm_back(middle, ffn_inverse, ffn_gain, ffn_grad)
    attended_low = middle_grad.astype(bf16)

    def middle_hook(s, moving):
        if s == 2:
            held["m11"] = weight_ring.begin(after(parts11, moving), halves)
        if s == 3:
            moving, held["y"] = tie(moving, produced)
        if s == ring.half:
            moving, held["m11"] = tie(moving, held["m11"])
        return moving


    attended_blocks = ring.gather(attended_low, True, middle_hook)
    expert_out = far_sum(held["y"], attended_blocks[-1])
    sum01 = weight_ring.finish(parts01, m01, halves, first=3)
    first_sum = jnp.concatenate([sum00, sum01], axis=1)
    first_home = uncross(after(first_sum, attended_blocks[-1]))
    second_moving = weight_ring.added(after(parts11, attended_blocks[-1]), held["m11"], 2)
    second_moving = weight_ring.hop(second_moving)
    raw_grad, attn_gain_grad, head_gain_grad, *normed_part = in_vmem(
        functools.partial(attention_back_kernel, len(token_blocks), heads, tile),
        [((sequence, 3 * wide), bf16), ((1, model), f32), ((2, HEAD_DIM), f32)]
        + [(block.shape, bf16) for block in token_blocks],
        [*attended_blocks, *token_blocks, qkv_weight, out_weight, *gains, *tables, *segments]
        + [inverse_all, raw, low, log_total],
        8 * sequence * wide * (4 * model + 5 * sequence),
        [pltpu.VMEM((sequence, wide), dtype) for dtype in (bf16, f32, f32, f32)],
    )
    due = (normed_part, raw_grad, attn_gain_grad, head_gain_grad)
    due, second_moving, expert_out, first_home = tie(
        due, second_moving, expert_out, first_home
    )
    normed_part, raw_grad, attn_gain_grad, head_gain_grad = due
    final_stream = middle + expert_out
    output = final_stream.astype(bf16)
    query_gain_grad, key_gain_grad = head_gain_grad[0], head_gain_grad[1]
    router_size = experts * model
    squares = jnp.stack(
        [jnp.sum(v * v) for v in (middle, final_stream, attended, expert_out)]
    )
    small = Sum(
        jnp.concatenate(
            [
                router_grad.reshape(-1),
                ffn_gain_grad,
                attn_gain_grad[0],
                query_gain_grad,
                key_gain_grad,
                jnp.pad(squares, (0, 124)),
            ]
        ).reshape(-1, 128)
    )

    qkv_grad = mm(normed_all, raw_grad, TN).astype(bf16)
    qkv_grad = qkv_grad.reshape(shards, owners, quarter, 3 * wide).transpose(1, 0, 2, 3)
    fold = Fold(qkv_grad, "expert")
    held["fold"] = fold.send()

    def normed_hook(s, moving):
        if s <= ring.half:
            if s != 3:
                small.step()
            moving, small.total = tie(moving, small.step())
        if s in (2, 3) and held["fold"] is not None:
            moving, came = tie(moving, held["fold"])
            fold.add(came)
            held["fold"] = fold.send() if fold.left else None
        if s == 2:
            held["n2"] = moving
        if s == ring.half:
            held["n4"] = moving
        if s == ring.half + 1:
            held["end"] = moving
        return moving

    normed_grad = ring.finish(normed_part, ring.begin(normed_part, True), True, hook=normed_hook)
    tokens_grad = (
        middle_grad + norm_back(stream, inverse_all[:rows], attn_gain, normed_grad)
    ).astype(bf16)
    if held["fold"] is not None:
        fold.add(held["fold"])
    qkv_grad = fold.finish()
    qkv_grad = lax.all_to_all(qkv_grad, "wshard", split_axis=0, concat_axis=0, tiled=True)
    qkv_grad = gather_bits(qkv_grad, "expert")
    query_weight_grad, key_weight_grad, value_weight_grad = in_vmem(
        spread_kernel, [((owners * quarter, model), f32)] * 3, [qkv_grad], 0
    )
    out_grad = mm(mixed, after(jnp.concatenate(attended_blocks, axis=0), held["n4"]), TN)
    out_grad = Fold(out_grad.astype(bf16).reshape(owners, -1, model), "expert").finish()
    out_grad = gather_bits(out_grad, "expert").reshape(-1, model).astype(f32)

    second_sum = jnp.concatenate(
        [
            weight_ring.finish(parts, moving, halves, first=3)
            for parts, moving in ((parts10, m10), (parts11, second_moving))
        ],
        axis=1,
    )
    second_home = uncross(after(second_sum, held["end"]))
    if split == 2:
        flag = jnp.where(upper, 1, 0).astype(jnp.int32)[None]
        pairs = [first_sum[: 3 * depth], first_home, second_sum[: 3 * depth], second_home]
        hidden = gate_weight.shape[2]
        wide_shape, tall_shape = (local_experts, depth, hidden), (local_experts, hidden, depth)
        gate_weight_grad, up_weight_grad, down_weight_grad = in_vmem(
            merge_kernel,
            [(wide_shape, f32), (wide_shape, f32), (tall_shape, f32)],
            [flag, *pairs],
            0,
            scalars=1,
        )
    else:
        summed = (first_sum, second_sum)
        gate_weight_grad = jnp.stack([s[:depth] for s in summed])
        up_weight_grad = jnp.stack([s[depth : 2 * depth] for s in summed])
        down_weight_grad = jnp.stack([s[2 * depth :].T for s in summed])

    small_sums = small.finish().reshape(-1)
    sizes = [router_size, model, model, HEAD_DIM, HEAD_DIM, 4]
    starts = [sum(sizes[:k]) for k in range(len(sizes))]
    router_sum, ffn_gain_grad, attn_gain_grad, query_gain_grad, key_gain_grad, squares = [
        small_sums[a : a + b] for a, b in zip(starts, sizes)
    ]
    router_weight_grad = router_sum.reshape(experts, model).T
    stream_rms = jnp.sqrt(squares / (rows * owners * shards * model))
    return (
        output,
        tokens_grad,
        attn_gain_grad,
        query_weight_grad,
        key_weight_grad,
        value_weight_grad,
        out_grad,
        query_gain_grad,
        key_gain_grad,
        ffn_gain_grad,
        router_weight_grad,
        gate_weight_grad,
        up_weight_grad,
        down_weight_grad,
        stream_rms,
    )


def solution(mesh):
    rows = P(("expert", "wshard"), None)
    shard = P("wshard", None)
    wide = P("expert", "wshard", None)
    tall = P("expert", None, "wshard")
    return jax.shard_map(
        local,
        mesh=mesh,
        in_specs=(rows, P("expert"), rows, P(), shard, shard, shard, shard)
        + (P(), P(), P(), P(), wide, wide, tall, rows),
        out_specs=(rows, rows, P(), shard, shard, shard, shard)
        + (P(), P(), P(), P(), wide, wide, tall, P()),
        check_vma=False,
    )
```

```python
import functools
import math

import jax
import jax.numpy as jnp
from jax import lax
from jax.experimental import pallas as pl
from jax.experimental.pallas import tpu as pltpu
from jax.sharding import PartitionSpec as P

HEADS = 16
HEAD_DIM = 128
epsilon = 1e-06
rope_base = 50000.0
highest = lax.Precision.HIGHEST
bf16 = jnp.bfloat16
f32 = jnp.float32

NN = (((1,), (0,)), ((), ()))
NT = (((1,), (1,)), ((), ()))
TN = (((0,), (0,)), ((), ()))


def mm(a, b, dims=NN):
    return lax.dot_general(a, b, dims, preferred_element_type=f32)


def tie(*arrays):
    return lax.optimization_barrier(arrays)


def after(x, *others):
    return lax.optimization_barrier((x, others))[0]


def ring_order(n):
    return list(range(0, n, 2)) + list(range(n - 1, 0, -2))


class Ring:
    def __init__(self, axis, groups=1):
        self.axis = axis
        total = lax.axis_size(axis)
        n = total // groups
        order = ring_order(n)
        self.down = [
            (g * n + order[i], g * n + order[(i + 1) % n]) for g in range(groups) for i in range(n)
        ]
        self.up = [(b, a) for a, b in self.down]
        place = [order.index(w % n) for w in range(total)]
        here = jnp.asarray(place, jnp.int32)[lax.axis_index(axis)]
        self.half = n // 2
        self.offsets = [0]
        for s in range(1, self.half):
            self.offsets += [-s, s]
        self.offsets.append(-self.half)
        table = jnp.asarray(order, jnp.int32)
        first = lax.axis_index(axis) // n * n
        self.owner = first + table[(here + jnp.asarray(self.offsets, jnp.int32) + n) % n]

    def hop(self, moving):
        return {
            sign: lax.ppermute(block, self.axis, self.down if sign == 1 else self.up)
            for sign, block in moving.items()
        }

    def gather(self, own, halves=False, hook=None, first=None):
        got = {0: own}
        moving = {1: own, -1: own}
        for s in range(1, self.half + 1):
            if s == self.half:
                if halves:
                    middle = own.shape[0] // 2
                    moving = {1: moving[1][:middle], -1: moving[-1][middle:]}
                else:
                    moving.pop(-1)
            if hook:
                moving = hook(s, moving)
            moving = first if s == 1 and first else self.hop(moving)
            for sign, block in moving.items():
                got[-s * sign] = block
        blocks = [got[o] for o in self.offsets]
        return blocks + [moving[-1]] if halves else blocks

    def begin(self, parts, halves=False):
        moving = {1: parts[2 * self.half - 1]}
        if halves:
            moving[-1] = parts[-1]
        return self.hop(moving)

    def scatter(self, parts, halves=False, hook=None):
        return self.finish(parts, self.begin(parts, halves), halves, hook)

    def added(self, parts, moving, s):
        part = dict(zip(self.offsets, parts))
        distance = self.half - s + 1
        out = {}
        for sign in (1, -1):
            own = part[sign * distance]
            if sign not in moving:
                out[sign] = own
            elif moving[sign].shape == own.shape:
                out[sign] = (moving[sign].astype(f32) + own.astype(f32)).astype(bf16)
            else:
                middle = own.shape[0] // 2
                low, high = own[:middle], own[middle:]
                if sign == 1:
                    low = (moving[sign].astype(f32) + low.astype(f32)).astype(bf16)
                else:
                    high = (moving[sign].astype(f32) + high.astype(f32)).astype(bf16)
                out[sign] = jnp.concatenate([low, high], axis=0)
        return out

    def finish(self, parts, moving, halves=False, hook=None, first=2):
        for s in range(first, self.half + 1):
            moving = self.added(parts, moving, s)
            if hook:
                moving = hook(s, moving)
            moving = self.hop(moving)
        if hook:
            moving = hook(self.half + 1, moving)
        total = parts[0].astype(f32)
        for block in moving.values():
            total = total + block.astype(f32)
        return total


def bits_of(size):
    return [1 << b for b in range(size.bit_length() - 1)]


def swap(x, axis, bit):
    return lax.ppermute(x, axis, [(i, i ^ bit) for i in range(lax.axis_size(axis))])


def gather_bits(x, axis, holds=()):
    index = lax.axis_index(axis)
    out = x[None]
    for k, bit in enumerate(reversed(bits_of(lax.axis_size(axis)))):
        came = swap(out, axis, bit)
        if k < len(holds):
            came = after(came, holds[k])
        high = (index & bit) != 0
        out = jnp.stack([jnp.where(high, came, out), jnp.where(high, out, came)], axis=1)
        out = out.reshape((-1,) + x.shape)
    return out


class Fold:
    def __init__(self, x, axis):
        self.x, self.axis = x, axis
        self.left = bits_of(lax.axis_size(axis))

    def send(self):
        pairs = self.x.reshape((-1, 2) + self.x.shape[1:])
        bit = self.left.pop(0)
        high = (lax.axis_index(self.axis) & bit) != 0
        self.keep = jnp.where(high, pairs[:, 1], pairs[:, 0])
        return swap(jnp.where(high, pairs[:, 0], pairs[:, 1]), self.axis, bit)

    def add(self, came):
        self.x = (self.keep.astype(f32) + came.astype(f32)).astype(bf16)

    def finish(self):
        while self.left:
            self.add(self.send())
        return self.x[0]


class Sum:
    def __init__(self, x):
        self.total = x
        self.left = [
            (axis, bit)
            for axis in ("expert", "wshard")
            for bit in reversed(bits_of(lax.axis_size(axis)))
        ]

    def step(self):
        if self.left:
            self.total = self.total + swap(self.total, *self.left.pop(0))
        return self.total

    def finish(self):
        while self.left:
            self.step()
        return self.total


class Group:
    def __init__(self, split):
        self.owners = lax.axis_size("expert")
        self.split = split
        self.far = lax.axis_size("wshard") // 2
        self.rel = [0]
        for bit in reversed(bits_of(self.owners)):
            self.rel += [r ^ bit for r in self.rel]

    def far_block(self, x):
        return [swap(x, "wshard", self.far)] if self.split == 2 else []

    def join(self, own, far):
        if far:
            own = [block for pair in zip(own, far) for block in pair]
        return jnp.concatenate(own, axis=0)

    def gather(self, x, hook=None):
        blocks = [x]
        for bit in reversed(bits_of(self.owners)):
            came = [swap(b, "expert", bit) for b in blocks]
            if hook:
                came = hook(came)
            blocks += came
        return blocks

    def begin(self, send):
        return swap(send, "expert", 1)

    def scatter(self, keep, send=None, came=None):
        bits = bits_of(self.owners)
        came = self.begin(send) if came is None else came
        x = keep.astype(f32) + came.astype(f32)
        for bit in bits[1:]:
            half = x.shape[0] // 2
            size = half // self.split if bit == bits[-1] else half
            parts = []
            for start in reversed(range(0, half, size)):
                part = x[half + start : half + start + size].astype(bf16)
                parts.append(x[start : start + size] + swap(part, "expert", bit).astype(f32))
            x = parts[0] if len(parts) == 1 else parts[::-1]
        return x if isinstance(x, list) else [x]


def expert_kernel(expert, turn, first, last, n, owner, m_ref, x_hbm, g_hbm, *refs):
    weights, refs = refs[:n], refs[n:]
    before, refs = ((), refs) if first else (refs[:2], refs[2:])
    state_ref, refs = refs[0], refs[1:]
    k = 2 if last else 1
    ends, refs = (refs[:k], refs[k : 2 * k]), refs[2 * k :]
    grads, refs = refs[:n], refs[n:]
    x_ref, g_ref, y_ref, dx_ref, w_ref, d_ref, mixed_ref, gate_ref, up_ref = refs[:9]
    old_refs = refs[9:11]
    in_sem, w_sem, end_sem, d_sem, old_sem = refs[11:]
    rows, model = x_ref.shape
    width = w_ref.shape[1]
    count = owner.shape[0] - 1
    depth = model // count
    tile = min(rows, 512)
    starts = [sum(w.shape[0] for w in weights[:j]) for j in range(n)] + [w_ref.shape[0]]
    places = []
    for k in range(count):
        at = pl.ds(pl.multiple_of(owner[k] * depth, depth), depth)
        places.append((at, [pl.ds((3 * k + part) * depth, depth) for part in range(3)]))
    source = {start // (3 * depth): j for j, start in enumerate(starts[:-1])}
    final = {start // (3 * depth) - 1: j for j, start in enumerate(starts[1:])}
    copy = pltpu.make_async_copy

    def fetch(k, what):
        at = pl.ds(k * tile, tile)
        from_hbm, to = ((x_hbm, x_ref), (g_hbm, g_ref))[what]
        return copy(from_hbm.at[at], to.at[at], in_sem.at[what, k])

    def fetch_weight(j):
        here = pl.ds(starts[j], weights[j].shape[0])
        return copy(weights[j].at[:, pl.ds(turn * width, width)], w_ref.at[here], w_sem.at[j])

    def finish(k):
        at = places[k][0] if k < count else pl.ds(model, 128)
        copies = []
        for what, (ref, parts) in enumerate(zip((y_ref, dx_ref), ends)):
            half = rows // len(parts)
            for e, to in enumerate(parts):
                if k < count or what == 1:
                    rows_at = pl.ds(e * half, half)
                    sem = end_sem.at[2 * what + e, k]
                    copies.append(copy(ref.at[rows_at, at], to.at[:, at], sem))
        return copies

    def put(j):
        here = pl.ds(starts[j], weights[j].shape[0])
        return copy(d_ref.at[here], grads[j], d_sem.at[j])

    for what in range(2):
        fetch(0, what).start()
    for j in range(n):
        fetch_weight(j).start()
    for k in range(1, rows // tile):
        for what in range(2):
            fetch(k, what).start()

    for what, old in enumerate(before):
        copy(old, old_refs[what], old_sem.at[what]).start()

    for start in range(0, rows, tile):
        here = pl.ds(start, tile)
        for what in range(2):
            fetch(start // tile, what).wait()
        gate = up = back = logits = None
        for k, (at, parts) in enumerate(places):
            if start == 0 and k in source:
                fetch_weight(source[k]).wait()
            x, g = x_ref[here, at], g_ref[here, at]
            a, b, c = mm(x, w_ref[parts[0]]), mm(x, w_ref[parts[1]]), mm(g, w_ref[parts[2]])
            gate, up, back = (a, b, c) if k == 0 else (gate + a, up + b, back + c)
            if first:
                a = mm(x, m_ref[at])
                logits = a if k == 0 else logits + a
        if first:
            named = g_ref[here, model:].astype(f32) > 0.0
            top = jnp.max(jnp.where(named, logits, -1e30), axis=1, keepdims=True)
            lifted = jnp.where(named, jnp.exp(jnp.minimum(logits - top, 0.0)), 0.0)
            state = lifted * (1.0 / jnp.sum(lifted, axis=1, keepdims=True))
        else:
            state = m_ref[here]
        lanes = lax.broadcasted_iota(jnp.int32, state.shape, 1)
        lane = owner[count] + expert
        mix = jnp.sum(jnp.where(lanes == lane, state, 0.0), axis=1, keepdims=True)
        sig = 1.0 / (1.0 + jnp.exp(-gate))
        act = gate * sig
        hidden = act * up
        mixing_grad = jnp.sum(hidden * back, axis=1, keepdims=True)
        state = state + jnp.where(lanes == 64 + lane, mixing_grad, 0.0)
        state_ref[here] = state
        if last:
            state = jnp.where(lanes >= 64, state, 0.0)
            near = state.astype(bf16).astype(f32)
            dx_ref[here, model:] = (near + pltpu.roll(state - near, 32, 1)).astype(bf16)
        mixed_ref[here] = (mix * hidden).astype(bf16)
        hidden_grad = mix * back
        gate_ref[here] = (hidden_grad * up * sig * (1.0 + gate * (1.0 - sig))).astype(bf16)
        up_ref[here] = (hidden_grad * act).astype(bf16)
    for what, old in enumerate(before):
        copy(old, old_refs[what], old_sem.at[what]).wait()
    mixed, gate_grad, up_grad = mixed_ref[...], gate_ref[...], up_ref[...]
    for k, (at, parts) in enumerate(places):
        y = mm(mixed, w_ref[parts[2]], NT)
        dx = mm(gate_grad, w_ref[parts[0]], NT) + mm(up_grad, w_ref[parts[1]], NT)
        if before:
            y = y + old_refs[0][:, at].astype(f32)
            dx = dx + old_refs[1][:, at].astype(f32)
        y_ref[:, at], dx_ref[:, at] = y.astype(bf16), dx.astype(bf16)
        for end in finish(k):
            end.start()
        x, g = x_ref[:, at], g_ref[:, at]
        d_ref[parts[0]] = mm(x, gate_grad, TN).astype(bf16)
        d_ref[parts[1]] = mm(x, up_grad, TN).astype(bf16)
        d_ref[parts[2]] = mm(g, mixed, TN).astype(bf16)
        if k in final:
            put(final[k]).start()
    if last:
        for end in finish(count):
            end.start()
    for k in range(count + last):
        for end in finish(k):
            end.wait()
    for j in range(n):
        put(j).wait()


def expert_pass(expert, turn, first, last, turns, owner, x, g, mix, weights, before):
    n = len(weights)
    rows, model = x.shape
    deep, width = sum(w.shape[0] for w in weights), weights[0].shape[1] // turns
    anywhere, vmem = pl.BlockSpec(memory_space=pl.ANY), pl.BlockSpec(memory_space=pltpu.VMEM)
    count = owner.shape[0] - 1
    k = 2 if last else 1
    wide = model + 128 if last else model
    ends = [jax.ShapeDtypeStruct((rows // k, model), bf16)] * k
    ends += [jax.ShapeDtypeStruct((rows // k, wide), bf16)] * k
    old = pltpu.VMEM((8, 128) if first else (rows, model), bf16)
    out = pl.pallas_call(
        functools.partial(expert_kernel, expert, turn, first, last, n),
        in_specs=[pl.BlockSpec(memory_space=pltpu.SMEM), vmem]
        + [anywhere] * (2 + n + len(before)),
        out_specs=[vmem] + [anywhere] * (2 * k + n),
        scratch_shapes=[
            pltpu.VMEM((rows, model), bf16),
            pltpu.VMEM((rows, g.shape[1]), bf16),
            pltpu.VMEM((rows, model), bf16),
            pltpu.VMEM((rows, wide), bf16),
            pltpu.VMEM((deep, width), bf16),
            pltpu.VMEM((deep, width), bf16),
            pltpu.VMEM((rows, width), bf16),
            pltpu.VMEM((rows, width), bf16),
            pltpu.VMEM((rows, width), bf16),
            old,
            old,
            pltpu.SemaphoreType.DMA((2, -(-rows // 512))),
            pltpu.SemaphoreType.DMA((n,)),
            pltpu.SemaphoreType.DMA((4, count + 1)),
            pltpu.SemaphoreType.DMA((n,)),
            pltpu.SemaphoreType.DMA((2,)),
        ],
        out_shape=[jax.ShapeDtypeStruct((rows, 128), f32)]
        + ends
        + [jax.ShapeDtypeStruct((w.shape[0], width), bf16) for w in weights],
        compiler_params=pltpu.CompilerParams(vmem_limit_bytes=60 << 20),
        cost_estimate=pl.CostEstimate(
            flops=18 * rows * model * width, transcendentals=0, bytes_accessed=4 * deep * width
        ),
    )(owner, mix, x, g, *weights, *before)
    return out[0], list(out[1 : 1 + 2 * k]), list(out[1 + 2 * k :])


def spread_kernel(x_ref, *out_refs):
    owners, shards, rows, columns = x_ref.shape
    wide = columns // len(out_refs)
    for e in range(owners):
        for w in range(shards):
            for i, out_ref in enumerate(out_refs):
                part = x_ref[e, w, :, i * wide : (i + 1) * wide].astype(f32)
                out_ref[e * rows : (e + 1) * rows, w * wide : (w + 1) * wide] = part


def merge_kernel(upper_ref, *refs):
    gate_ref, up_ref, down_ref = refs[-3:]
    half = refs[0].shape[1]
    depth = gate_ref.shape[1]
    upper = upper_ref[0] > 0
    for i in range(gate_ref.shape[0]):
        for part, out_ref in enumerate((gate_ref, up_ref, down_ref)):
            rows = pl.ds(part * depth, depth)
            own, other = refs[2 * i][rows], refs[2 * i + 1][rows].astype(f32)
            low, high = jnp.where(upper, other, own), jnp.where(upper, own, other)
            if part < 2:
                out_ref[i, :, :half], out_ref[i, :, half:] = low, high
            else:
                out_ref[i, :half], out_ref[i, half:] = low.T, high.T


def inverse_rms(values):
    return lax.rsqrt(jnp.mean(values * values, axis=-1, keepdims=True) + epsilon)


def norm_back(values, inverse, gain_vector, grad_rows):
    scaled = values * inverse
    weighted = grad_rows * gain_vector
    return inverse * (weighted - scaled * jnp.mean(weighted * scaled, axis=-1, keepdims=True))


def rotate(values, cosine, sine):
    return values * cosine + pltpu.roll(values, HEAD_DIM // 2, 1) * sine


def each_block(count, size, body):
    def one(k, carry):
        body(pl.ds(pl.multiple_of(k * size, size), size))
        return carry

    lax.fori_loop(0, count // size, one, 0)


def row_places(refs):
    starts = [sum(ref.shape[0] for ref in refs[:b]) for b in range(len(refs))]
    return [pl.ds(start, ref.shape[0]) for start, ref in zip(starts, refs)]


def head_columns(h, part=0, heads=1):
    return pl.ds((part * heads + h) * HEAD_DIM, HEAD_DIM)


def scores_of(low_ref, seg_ref, segs_ref, here, h, heads):
    keys = low_ref[:, head_columns(h, 1, heads)]
    scores = mm(low_ref[here, head_columns(h)], keys, NT) * (1.0 / math.sqrt(HEAD_DIM))
    return jnp.where(seg_ref[here] == segs_ref[...], scores, -1e30)


def attention_kernel(n, heads, block, *refs):
    tokens, refs = refs[:n], refs[n:]
    w_ref, out_ref, gain_ref, qg_ref, kg_ref, cos_ref, sin_ref, seg_ref, segs_ref = refs[:9]
    normed_ref, inverse_ref, raw_ref, low_ref, lse_ref, mixed_ref = refs[9:15]
    parts = refs[15:]
    places = row_places(tokens)
    wide = heads * HEAD_DIM
    for b, here in enumerate(places):
        x = tokens[b][...].astype(f32)
        inverse = inverse_rms(x)
        inverse_ref[here] = inverse
        normed_ref[here] = (x * inverse * gain_ref[...]).astype(bf16)

    def project(here):
        raw = mm(normed_ref[here], w_ref[...])
        raw_ref[here] = raw[:, : 2 * wide]
        low_ref[here, 2 * wide :] = raw[:, 2 * wide :].astype(bf16)
        for part, g_ref in ((0, qg_ref), (1, kg_ref)):
            for h in range(heads):
                at = (part * heads + h) * HEAD_DIM
                u = raw[:, at : at + HEAD_DIM]
                u = u * inverse_rms(u) * g_ref[...]
                low_ref[here, at : at + HEAD_DIM] = rotate(u, cos_ref[here], sin_ref[here]).astype(bf16)

    count = normed_ref.shape[0]
    each_block(count, block, project)

    def attend(here):
        for h in range(heads):
            scores = scores_of(low_ref, seg_ref, segs_ref, here, h, heads)
            top = jnp.max(scores, axis=-1, keepdims=True)
            lifted = jnp.exp(scores - top)
            total = jnp.sum(lifted, axis=-1, keepdims=True)
            probs = (lifted * (1.0 / total)).astype(bf16)
            lse_ref[here, h : h + 1] = top + jnp.log(total)
            mixed_ref[here, head_columns(h)] = mm(
                probs, low_ref[:, head_columns(h, 2, heads)]
            ).astype(bf16)

    each_block(count, block, attend)
    for b, here in enumerate(places):
        parts[b][...] = mm(mixed_ref[here], out_ref[...]).astype(bf16)


def attention_back_kernel(n, heads, block, *refs):
    grads, tokens, refs = refs[:n], refs[n : 2 * n], refs[2 * n :]
    w_ref, out_ref, qg_ref, kg_ref, cos_ref, sin_ref, seg_ref, segs_ref = refs[:8]
    inverse_ref, raw_ref, low_ref, lse_ref = refs[8:12]
    raw_grad_ref, gain_ref, head_gain_ref = refs[12:15]
    parts, refs = refs[15 : 15 + n], refs[15 + n :]
    mixed_ref, query_ref, key_ref, value_ref = refs
    places = row_places(tokens)
    wide = heads * HEAD_DIM
    scale = 1.0 / math.sqrt(HEAD_DIM)
    for b, here in enumerate(places):
        mixed_ref[here] = mm(grads[b][...], out_ref[...], NT).astype(bf16)
    key_ref[...] = jnp.zeros_like(key_ref)
    value_ref[...] = jnp.zeros_like(value_ref)

    def attend(here):
        for h in range(heads):
            at = head_columns(h)
            scores = scores_of(low_ref, seg_ref, segs_ref, here, h, heads)
            probs = jnp.exp(scores - lse_ref[here, h : h + 1])
            mixed_grad = mixed_ref[here, at]
            probs_grad = mm(mixed_grad, low_ref[:, head_columns(h, 2, heads)], NT)
            mean = jnp.sum(probs * probs_grad, axis=-1, keepdims=True)
            scores_grad = (probs * (probs_grad - mean)).astype(bf16)
            query_ref[here, at] = mm(scores_grad, low_ref[:, head_columns(h, 1, heads)]) * scale
            key_ref[:, at] += mm(scores_grad, low_ref[here, at], TN) * scale
            value_ref[:, at] += mm(probs.astype(bf16), mixed_grad, TN)

    count = mixed_ref.shape[0]
    each_block(count, block, attend)
    head_gain_ref[...] = jnp.zeros_like(head_gain_ref)

    def norms_back(here):
        raw_grad_ref[here, 2 * wide :] = value_ref[here].astype(bf16)
        for part, g_ref, rot_ref in ((0, qg_ref, query_ref), (1, kg_ref, key_ref)):
            for h in range(heads):
                at = (part * heads + h) * HEAD_DIM
                grad = rotate(rot_ref[here, head_columns(h)], cos_ref[here], -sin_ref[here])
                u = raw_ref[here, at : at + HEAD_DIM]
                inverse = inverse_rms(u)
                head_gain_ref[part : part + 1] += jnp.sum(
                    grad * (u * inverse), axis=0, keepdims=True
                )
                raw_grad_ref[here, at : at + HEAD_DIM] = norm_back(
                    u, inverse, g_ref[...], grad
                ).astype(bf16)

    each_block(count, block, norms_back)
    gain = None
    for b, here in enumerate(places):
        part = mm(raw_grad_ref[here], w_ref[...], NT)
        parts[b][...] = part.astype(bf16)
        scaled = tokens[b][...].astype(f32) * inverse_ref[here]
        one = jnp.sum(part * scaled, axis=0, keepdims=True)
        gain = one if gain is None else gain + one
    gain_ref[...] = gain


def in_vmem(kernel, shapes, arrays, flops, scratch=(), scalars=0):
    return pl.pallas_call(
        kernel,
        in_specs=[pl.BlockSpec(memory_space=pltpu.SMEM)] * scalars
        + [pl.BlockSpec(memory_space=pltpu.VMEM)] * (len(arrays) - scalars),
        out_specs=[pl.BlockSpec(memory_space=pltpu.VMEM)] * len(shapes),
        out_shape=[jax.ShapeDtypeStruct(*shape) for shape in shapes],
        scratch_shapes=list(scratch),
        compiler_params=pltpu.CompilerParams(vmem_limit_bytes=60 << 20),
        cost_estimate=pl.CostEstimate(
            flops=flops,
            transcendentals=0,
            bytes_accessed=sum(a.size * a.dtype.itemsize for a in arrays),
        ),
    )(*arrays)


def local(
    tokens,
    segment_ids,
    routes,
    attn_gain,
    query_weight,
    key_weight,
    value_weight,
    out_weight,
    query_gain,
    key_gain,
    ffn_gain,
    router_weight,
    gate_weight,
    up_weight,
    down_weight,
    d_output,
):
    rows, model = tokens.shape
    owners, shards = lax.axis_size("expert"), lax.axis_size("wshard")
    rank = lax.axis_index("expert")
    local_experts = gate_weight.shape[0]
    experts = local_experts * owners
    heads = HEADS // shards
    wide = heads * HEAD_DIM
    ring = Ring("wshard")
    split = 2 if rows * owners <= 512 else 1
    far = shards // split
    group = Group(split)
    weight_ring = Ring("wshard", split)
    upper = lax.axis_index("wshard") >= far

    held = {}
    quarter = query_weight.shape[0] // owners
    own_rows = jnp.concatenate(
        [
            lax.dynamic_slice_in_dim(w, rank * quarter, quarter)
            .reshape(quarter, shards, wide)
            .transpose(1, 0, 2)
            for w in (query_weight, key_weight, value_weight)
        ],
        axis=2,
    )
    own_columns = lax.all_to_all(own_rows, "wshard", split_axis=0, concat_axis=0, tiled=True)
    named = jnp.sum(
        (routes[:, :, None] == jnp.arange(128, dtype=jnp.int32)).astype(bf16), axis=1
    )
    grad_rows = jnp.concatenate([d_output, named], axis=1)

    def token_hook(s, moving):
        if s == 3:
            moving, held["columns"] = tie(moving, own_columns)
            held["two"] = moving
        if s == ring.half:
            held["last"] = moving
        return moving

    token_blocks = ring.gather(tokens, True, token_hook)
    qkv_weight = gather_bits(held["columns"], "expert", [held["last"]])
    qkv_weight = qkv_weight.transpose(1, 0, 2, 3).reshape(model, 3 * wide)
    grad_own = group.gather(after(grad_rows, held["two"]))

    weights, _ = tie((gate_weight, up_weight, down_weight), held["two"])
    packed = [
        jnp.concatenate([weights[0][i], weights[1][i], weights[2][i].T], axis=0)
        for i in range(local_experts)
    ]
    half = packed[0].shape[1] // 2

    def cross(i, start):
        if split == 1:
            return packed[i][:0]
        send = jnp.where(upper, packed[i][:, :half], packed[i][:, half:])
        return swap(after(send, start), "wshard", far)

    def crossed(i, came):
        if split == 1:
            return packed[i]
        return jnp.concatenate(
            [jnp.where(upper, packed[i][:, half:], packed[i][:, :half]), came], axis=0
        )

    halves = split == 2
    block_owner = weight_ring.owner
    if split == 2:
        block_owner = jnp.stack([block_owner, block_owner ^ far], axis=1).reshape(-1)
    cross_first, cross_second = cross(0, token_blocks[-1]), cross(1, token_blocks[-1])

    sequence = rows * shards
    position = (ring.owner[:, None] * rows + jnp.arange(rows, dtype=jnp.int32)).reshape(-1)
    frequency = rope_base ** (-2.0 * jnp.arange(HEAD_DIM // 2, dtype=f32) / HEAD_DIM)
    angles = position.astype(f32)[:, None] * frequency[None, :]
    cosine, sine = jnp.cos(angles), jnp.sin(angles)
    tables = (
        jnp.concatenate([cosine, cosine], axis=1),
        jnp.concatenate([-sine, sine], axis=1),
    )
    segments = segment_ids.reshape(shards, rows)[ring.owner].reshape(-1)
    segments = (segments[:, None], segments[None, :])
    gains = (query_gain[None], key_gain[None])
    tile = 256
    normed_all, inverse_all, raw, low, log_total, mixed, *attended_part = in_vmem(
        functools.partial(attention_kernel, len(token_blocks), heads, tile),
        [
            ((sequence, model), bf16),
            ((sequence, 1), f32),
            ((sequence, 2 * wide), f32),
            ((sequence, 3 * wide), bf16),
            ((sequence, heads), f32),
            ((sequence, wide), bf16),
        ]
        + [(block.shape, bf16) for block in token_blocks],
        [*token_blocks, qkv_weight, out_weight, attn_gain[None], *gains, *tables, *segments],
        8 * sequence * wide * (4 * model + 2 * sequence),
    )
    attended_part, cross_first, cross_second, grad_own = tie(
        attended_part, cross_first, cross_second, grad_own
    )
    grad_far = group.far_block(after(grad_rows, attended_part[0]))
    first_block = crossed(0, cross_first)
    last_hop = weight_ring.half

    def attended_hook(s, moving):
        if s == 2:
            held["a2"] = moving
            held["send"] = after(first_block, moving)
            if last_hop == 2:
                held["near"] = weight_ring.hop({1: held["send"], -1: held["send"]})
        if s == 3:
            moving, held["grad"] = tie(moving, grad_far)
        if s == ring.half:
            moving, held["near"] = tie(moving, held.get("near"))
        return moving

    attended = ring.finish(
        attended_part, ring.begin(attended_part, True), True, hook=attended_hook
    )
    near = 2 * weight_ring.half - 1
    grad_far = [b for block in held["grad"] for b in group.gather(block)]

    stream = tokens.astype(f32)
    middle = stream + attended
    ffn_inverse = inverse_rms(middle)
    ffn_low = (middle * ffn_inverse * ffn_gain).astype(bf16)

    ffn_far = group.far_block(ffn_low)
    ffn_own = group.gather(ffn_low)
    first_weights = weight_ring.gather(held["send"], halves, first=held["near"])
    ffn_far, first_weights[near:] = tie(ffn_far, first_weights[near:])
    second_block = crossed(1, after(cross_second, ffn_far or ffn_low))
    second_near = weight_ring.hop({1: second_block, -1: second_block})
    ffn_far = [b for block in ffn_far for b in group.gather(block)]
    ffn_all = group.join(ffn_own, ffn_far)
    grad_and_names = group.join(grad_own, grad_far)
    ffn_all, first_weights = tie(ffn_all, first_weights)
    router = jnp.pad(router_weight, ((0, 0), (0, 128 - experts)))
    block_owner = jnp.concatenate([block_owner, rank[None] * local_experts])
    depth = gate_weight.shape[1]

    def uncross(total):
        if split == 1:
            return total[:0]
        return swap(total[3 * depth :].astype(bf16), "wshard", far)

    turns = 2
    call = functools.partial(expert_pass, owner=block_owner, x=ffn_all, g=grad_and_names)

    def part_call(expert, turn, mix, weights, *before):
        first, last = (expert, turn) == (0, 0), (expert, turn) == (local_experts - 1, turns - 1)
        return call(expert, turn, first, last, turns, mix=mix, weights=weights, before=before)

    (state, ends, parts00), second_near = tie(
        part_call(0, 0, router, first_weights), second_near
    )
    second_weights = weight_ring.gather(second_block, halves, first=second_near)
    m00 = weight_ring.begin(parts00, halves)
    (state, ends, parts01), second_weights, m00 = tie(
        part_call(0, 1, state, first_weights, *ends), second_weights, m00
    )
    m00 = weight_ring.hop(weight_ring.added(parts00, m00, 2))
    m01 = weight_ring.begin(parts01, halves)
    (state, ends, parts10), m00, m01 = tie(
        part_call(1, 0, state, second_weights, *ends), m00, m01
    )
    m01 = weight_ring.hop(weight_ring.added(parts01, m01, 2))
    m10 = weight_ring.begin(parts10, halves)
    (state, ends, parts11), m01, m10 = tie(
        part_call(1, 1, state, second_weights, *ends), m01, m10
    )
    sum00 = weight_ring.finish(parts00, m00, halves, first=3)
    m10 = weight_ring.hop(weight_ring.added(parts10, m10, 2))
    came = group.begin(ends[3])
    y_came = group.begin(after(ends[1], came))
    row_grads = group.scatter(ends[2], came=came)
    row_grads[-1], m10 = tie(row_grads[-1], m10)
    produced = group.scatter(after(ends[0], row_grads[-1]), came=y_came)

    def far_sum(blocks, hold):
        if split == 1:
            return blocks[0]
        send = after(blocks[1].astype(bf16), hold)
        return blocks[0] + swap(send, "wshard", far).astype(f32)

    ffn_grad = far_sum(row_grads, came)
    mixing_grad = ffn_grad[:, model + 64 : model + 64 + experts]
    mixing_grad = mixing_grad + ffn_grad[:, model + 96 : model + 96 + experts]
    ffn_grad = ffn_grad[:, :model]
    mixing_own = state[:rows, :experts]
    logits_grad = mixing_own * (
        mixing_grad - jnp.sum(mixing_own * mixing_grad, axis=1, keepdims=True)
    )
    router_grad = lax.dot_general(
        logits_grad, ffn_low.astype(f32), TN, precision=highest, preferred_element_type=f32
    )
    ffn_grad = ffn_grad + lax.dot_general(
        logits_grad, router_weight.astype(f32), NT, precision=highest, preferred_element_type=f32
    )
    ffn_gain_grad = jnp.sum(ffn_grad * (middle * ffn_inverse), axis=0)
    middle_grad = d_output.astype(f32) + norm_back(middle, ffn_inverse, ffn_gain, ffn_grad)
    attended_low = middle_grad.astype(bf16)

    def middle_hook(s, moving):
        if s == 2:
            held["m11"] = weight_ring.begin(after(parts11, moving), halves)
        if s == 3:
            moving, held["y"] = tie(moving, produced)
        if s == ring.half:
            moving, held["m11"] = tie(moving, held["m11"])
        return moving


    attended_blocks = ring.gather(attended_low, True, middle_hook)
    far_rows = after(held["y"][-1].astype(bf16), attended_blocks[-1])
    expert_out = held["y"][0]
    if split == 2:
        expert_out = expert_out + swap(far_rows, "wshard", far).astype(f32)
    sum01 = weight_ring.finish(parts01, m01, halves, first=3)
    first_sum = jnp.concatenate([sum00, sum01], axis=1)
    first_home = uncross(after(first_sum, far_rows))
    second_moving = weight_ring.added(after(parts11, attended_blocks[-1]), held["m11"], 2)
    second_moving = weight_ring.hop(second_moving)
    raw_grad, attn_gain_grad, head_gain_grad, *normed_part = in_vmem(
        functools.partial(attention_back_kernel, len(token_blocks), heads, tile),
        [((sequence, 3 * wide), bf16), ((1, model), f32), ((2, HEAD_DIM), f32)]
        + [(block.shape, bf16) for block in token_blocks],
        [*attended_blocks, *token_blocks, qkv_weight, out_weight, *gains, *tables, *segments]
        + [inverse_all, raw, low, log_total],
        8 * sequence * wide * (4 * model + 5 * sequence),
        [pltpu.VMEM((sequence, wide), dtype) for dtype in (bf16, f32, f32, f32)],
    )
    due = (normed_part, raw_grad, attn_gain_grad, head_gain_grad)
    due, second_moving, expert_out, first_home = tie(
        due, second_moving, expert_out, first_home
    )
    normed_part, raw_grad, attn_gain_grad, head_gain_grad = due
    final_stream = middle + expert_out
    output = final_stream.astype(bf16)
    query_gain_grad, key_gain_grad = head_gain_grad[0], head_gain_grad[1]
    router_size = experts * model
    squares = jnp.stack(
        [jnp.sum(v * v) for v in (middle, final_stream, attended, expert_out)]
    )
    small = Sum(
        jnp.concatenate(
            [
                router_grad.reshape(-1),
                ffn_gain_grad,
                attn_gain_grad[0],
                query_gain_grad,
                key_gain_grad,
                jnp.pad(squares, (0, 124)),
            ]
        ).reshape(-1, 128)
    )

    qkv_grad = mm(normed_all, raw_grad, TN).astype(bf16)
    qkv_grad = qkv_grad.reshape(shards, owners, quarter, 3 * wide).transpose(1, 0, 2, 3)
    fold = Fold(qkv_grad, "expert")
    held["fold"] = fold.send()

    def normed_hook(s, moving):
        if s <= ring.half:
            if s != 3:
                small.step()
            moving, small.total = tie(moving, small.step())
        if s in (2, 3) and held["fold"] is not None:
            if s == 2:
                moving, came = tie(moving, held["fold"])
            else:
                came = after(held["fold"], moving)
            fold.add(came)
            held["fold"] = fold.send() if fold.left else None
        if s == 2:
            held["n2"] = moving
        if s == ring.half:
            held["n4"] = moving
        if s == ring.half + 1:
            held["end"] = moving
        return moving

    normed_grad = ring.finish(normed_part, ring.begin(normed_part, True), True, hook=normed_hook)
    tokens_grad = (
        middle_grad + norm_back(stream, inverse_all[:rows], attn_gain, normed_grad)
    ).astype(bf16)
    if held["fold"] is not None:
        fold.add(held["fold"])
    qkv_grad = fold.finish()
    qkv_grad = lax.all_to_all(qkv_grad, "wshard", split_axis=0, concat_axis=0, tiled=True)
    qkv_grad = gather_bits(qkv_grad, "expert")
    query_weight_grad, key_weight_grad, value_weight_grad = in_vmem(
        spread_kernel, [((owners * quarter, model), f32)] * 3, [qkv_grad], 0
    )
    out_grad = mm(mixed, after(jnp.concatenate(attended_blocks, axis=0), held["n4"]), TN)
    out_grad = Fold(out_grad.astype(bf16).reshape(owners, -1, model), "expert").finish()
    out_grad = gather_bits(out_grad, "expert").reshape(-1, model).astype(f32)

    second_sum = jnp.concatenate(
        [
            weight_ring.finish(parts, moving, halves, first=3)
            for parts, moving in ((parts10, m10), (parts11, second_moving))
        ],
        axis=1,
    )
    second_home = uncross(after(second_sum, held["end"]))
    if split == 2:
        flag = jnp.where(upper, 1, 0).astype(jnp.int32)[None]
        pairs = [first_sum[: 3 * depth], first_home, second_sum[: 3 * depth], second_home]
        hidden = gate_weight.shape[2]
        wide_shape, tall_shape = (local_experts, depth, hidden), (local_experts, hidden, depth)
        gate_weight_grad, up_weight_grad, down_weight_grad = in_vmem(
            merge_kernel,
            [(wide_shape, f32), (wide_shape, f32), (tall_shape, f32)],
            [flag, *pairs],
            0,
            scalars=1,
        )
    else:
        summed = (first_sum, second_sum)
        gate_weight_grad = jnp.stack([s[:depth] for s in summed])
        up_weight_grad = jnp.stack([s[depth : 2 * depth] for s in summed])
        down_weight_grad = jnp.stack([s[2 * depth :].T for s in summed])

    small_sums = small.finish().reshape(-1)
    sizes = [router_size, model, model, HEAD_DIM, HEAD_DIM, 4]
    starts = [sum(sizes[:k]) for k in range(len(sizes))]
    router_sum, ffn_gain_grad, attn_gain_grad, query_gain_grad, key_gain_grad, squares = [
        small_sums[a : a + b] for a, b in zip(starts, sizes)
    ]
    router_weight_grad = router_sum.reshape(experts, model).T
    stream_rms = jnp.sqrt(squares / (rows * owners * shards * model))
    return (
        output,
        tokens_grad,
        attn_gain_grad,
        query_weight_grad,
        key_weight_grad,
        value_weight_grad,
        out_grad,
        query_gain_grad,
        key_gain_grad,
        ffn_gain_grad,
        router_weight_grad,
        gate_weight_grad,
        up_weight_grad,
        down_weight_grad,
        stream_rms,
    )


def solution(mesh):
    rows = P(("expert", "wshard"), None)
    shard = P("wshard", None)
    wide = P("expert", "wshard", None)
    tall = P("expert", None, "wshard")
    return jax.shard_map(
        local,
        mesh=mesh,
        in_specs=(rows, P("expert"), rows, P(), shard, shard, shard, shard)
        + (P(), P(), P(), P(), wide, wide, tall, rows),
        out_specs=(rows, rows, P(), shard, shard, shard, shard)
        + (P(), P(), P(), P(), wide, wide, tall, P()),
        check_vma=False,
    )
```
